512 devices in a mesh: frame: 8 (over y, core), row: 8 (over z_lo), col: 8 (over x, z_hi).
Axes of the slice: x: 4, y: 4, z: 16 (z_hi: 2, z_lo: 8; z = z_hi * 8 + z_lo), core: 2. Of those that a mesh axis runs over, the one named last changes fastest.
Arguments:
- frames_in: bfloat16 [32, 64, 64, 1024], P('frame', 'row', None, 'col'), may hold values from -6 to 6
- spatial_weight: bfloat16 [9, 1024, 1024], P(None, ('frame', 'row'), 'col'), may hold values from -0.0625 to 0.0625
- temporal_weight: bfloat16 [3, 1024, 1024], P(None, ('frame', 'row'), 'col'), may hold values from -0.109375 to 0.109375
- spatial_bias: float32 [1024], P('col'), may hold values from -3 to 3
- temporal_bias: float32 [1024], P('col'), may hold values from -3 to 3
- clip_id: int32 [32], replicated, may hold values from 0 to 7, as said below
Outputs:
- block_out: bfloat16 [32, 64, 64, 1024], P('frame', 'row', None, 'col')
The draws below stay inside these ranges and needn't reach their ends.
Inputs may be any that keep to these rules, and one draw needn't show every extreme that they name: `clip_id`: clip numbers of the frames in order, never falling; each clip has 1 to 7 frames and one has exactly 7.
All inputs are finite; a program needn't handle non-finite values.
Results may differ from the reference program's by a relative error of at most 0.01.
Values may be sent and summed in bfloat16 or wider, within the bound.
A program may use at most 64 MiB of HBM per device.

```python
import jax
import jax.numpy as jnp
from jax import lax

CHANNELS = 1024
HEIGHT = 64
WIDTH = 64
FR_DEV = 4
FRAMES = 32


def draw_clip_id(key, part):
    groups = FRAMES // FR_DEV
    offsets = jax.random.randint(jax.random.fold_in(key, 11), (groups,), 1, FR_DEV).astype(jnp.int32)
    offsets = offsets.at[1].set(FR_DEV - 1)
    starts = jnp.arange(groups, dtype=jnp.int32) * FR_DEV + offsets
    starts = starts.at[0].set(FRAMES + 1)
    places = jnp.arange(FRAMES, dtype=jnp.int32)
    return jnp.sum((places[:, None] >= starts[None, :]).astype(jnp.int32), axis=1).astype(jnp.int32)


def block_levels(key, shape, shards, least, largest):
    factor_of = 1.0
    for dim, blocks in shards:
        steps = jax.random.uniform(jax.random.fold_in(jax.random.fold_in(key, 6), dim), (blocks,), jnp.float32, least / len(shards), largest / len(shards))
        factor_of = factor_of * jnp.repeat(jnp.exp(steps), shape[dim] // blocks).reshape((-1,) + (1,) * (len(shape) - 1 - dim))
    return factor_of


def noise(own_key, dims, spread, bound, split=(), kind=jnp.bfloat16):
    array = spread * jax.random.normal(own_key, dims, jnp.float32)
    if split:
        array = array * block_levels(own_key, dims, split, -0.22, 0.18)
    return jnp.clip(array, -bound, bound).astype(kind)


def setup_inputs(seed: int = 0) -> dict:
    keys = jax.random.split(jax.random.key(seed), 7)
    frames_in = noise(keys[0], (FRAMES, HEIGHT, WIDTH, CHANNELS), 1.0, 6.0, ((0, 8), (1, 8), (3, 8)))
    spatial_weight = noise(keys[1], (9, CHANNELS, CHANNELS), (9 * CHANNELS) ** -0.5, 0.0625, ((1, 64), (2, 8)))
    temporal_weight = noise(keys[2], (3, CHANNELS, CHANNELS), (3 * CHANNELS) ** -0.5, 0.109375, ((1, 64), (2, 8)))
    spatial_bias = noise(keys[3], (CHANNELS,), 0.5, 3.0, ((0, 8),), jnp.float32)
    temporal_bias = noise(keys[4], (CHANNELS,), 0.5, 3.0, ((0, 8),), jnp.float32)
    clip_id = draw_clip_id(jax.random.fold_in(keys[6], 71), 0)
    return {"frames_in": frames_in, "spatial_weight": spatial_weight, "temporal_weight": temporal_weight, "spatial_bias": spatial_bias, "temporal_bias": temporal_bias, "clip_id": clip_id}


def reference(frames_in, spatial_weight, temporal_weight, spatial_bias, temporal_bias, clip_id):
    padded = jnp.pad(frames_in, ((0, 0), (1, 1), (1, 1), (0, 0)))

    def spatial_frame(frame):
        total = jnp.zeros((HEIGHT * WIDTH, CHANNELS), jnp.float32)
        for tap in range(9):
            shift_y, shift_x = tap // 3, tap % 3
            window = frame[shift_y:shift_y + HEIGHT, shift_x:shift_x + WIDTH, :].reshape(HEIGHT * WIDTH, CHANNELS)
            total = total + jnp.dot(window, spatial_weight[tap], preferred_element_type=jnp.float32)
        return total.reshape(HEIGHT, WIDTH, CHANNELS)

    spatial = lax.map(spatial_frame, padded)
    hidden = (spatial + spatial_bias).astype(jnp.bfloat16)
    active = jax.nn.silu(hidden.astype(jnp.float32)).astype(jnp.bfloat16)
    same = (clip_id[1:] == clip_id[:-1]).astype(jnp.float32)
    prev_ok = jnp.concatenate([jnp.zeros((1,), jnp.float32), same])
    next_ok = jnp.concatenate([same, jnp.zeros((1,), jnp.float32)])
    act_pad = jnp.pad(active, ((1, 1), (0, 0), (0, 0), (0, 0)))

    def temporal_frame(index):
        total = hidden[index].astype(jnp.float32).reshape(HEIGHT * WIDTH, CHANNELS) + temporal_bias
        weights_by_tap = (prev_ok[index], jnp.float32(1.0), next_ok[index])
        for tap in range(3):
            source = lax.dynamic_index_in_dim(act_pad, index + tap, 0, keepdims=False).reshape(HEIGHT * WIDTH, CHANNELS)
            term = jnp.dot(source, temporal_weight[tap], preferred_element_type=jnp.float32)
            total = total + weights_by_tap[tap] * term
        return total.reshape(HEIGHT, WIDTH, CHANNELS).astype(jnp.bfloat16)

    return lax.map(temporal_frame, jnp.arange(FRAMES, dtype=jnp.int32))
```

```python
import jax
import jax.numpy as jnp
from jax import lax
from jax.sharding import Mesh
from jax.sharding import PartitionSpec as P

FRAME = ("fy", "fc")
COL = ("cx", "cz")


def shift_halo(block, axis, count, dim, width):
    forward = [(i, i + 1) for i in range(count - 1)]
    backward = [(target, source) for source, target in forward]
    low = lax.ppermute(
        lax.slice_in_dim(block, block.shape[dim] - width, None, axis=dim), axis, forward
    )
    high = lax.ppermute(lax.slice_in_dim(block, 0, width, axis=dim), axis, backward)
    return jnp.concatenate([low, block, high], axis=dim)


def col_gather(block):
    partner = lax.ppermute(block, "cz", [(0, 1), (1, 0)])
    first = lax.axis_index("cz") == 0
    pair = jnp.where(
        first,
        jnp.concatenate([block, partner], axis=3),
        jnp.concatenate([partner, block], axis=3),
    )
    return lax.all_gather(pair, "cx", axis=3, tiled=True)


def weight_gather(weight):
    inner = lax.all_gather(weight, "row", axis=1, tiled=True)
    return lax.all_gather(inner, FRAME, axis=1, tiled=True)


def spatial_terms(total, gathered, weights):
    row_count = total.shape[1]
    wide = total.shape[2]
    for tap in range(9):
        shift_y, shift_x = (tap // 3, tap % 3)
        window = gathered[:, shift_y : shift_y + row_count, shift_x : shift_x + wide, :]
        total = total + jnp.einsum(
            "fhwc,cd->fhwd", window, weights[tap], preferred_element_type=jnp.float32
        )
    return total


def body(frames_in, spatial_weight, temporal_weight, spatial_bias, temporal_bias, clip_id):
    fr_count, row_count, wide, col_width = frames_in.shape
    full_spatial = weight_gather(spatial_weight)
    full_temporal = weight_gather(temporal_weight)
    rimmed = shift_halo(frames_in, "row", lax.axis_size("row"), 1, 1)
    gathered = col_gather(rimmed)
    gathered = jnp.pad(gathered, ((0, 0), (0, 0), (1, 1), (0, 0)))
    gathered, full_spatial, full_temporal = lax.optimization_barrier(
        (gathered, full_spatial, full_temporal)
    )
    blank = jnp.zeros((fr_count, row_count, wide, col_width), jnp.float32)
    spatial = spatial_terms(blank, gathered, full_spatial)
    hidden = (spatial + spatial_bias).astype(jnp.bfloat16)
    active = jax.nn.silu(hidden.astype(jnp.float32)).astype(jnp.bfloat16)
    index = lax.axis_index(FRAME)
    edge_ids = jnp.full((1,), -1, jnp.int32)
    padded_ids = jnp.concatenate([edge_ids, clip_id, edge_ids])
    local_ids = lax.dynamic_slice_in_dim(padded_ids, index * fr_count, fr_count + 2)
    prev_ok = (local_ids[1:-1] == local_ids[:-2]).astype(jnp.float32).reshape(fr_count, 1, 1, 1)
    next_ok = (local_ids[1:-1] == local_ids[2:]).astype(jnp.float32).reshape(fr_count, 1, 1, 1)
    source = shift_halo(active, FRAME, lax.axis_size(FRAME), 0, 1)
    whole = col_gather(source)
    taps = [
        jnp.einsum(
            "fhwc,cd->fhwd",
            whole[tap : tap + fr_count],
            full_temporal[tap],
            preferred_element_type=jnp.float32,
        )
        for tap in range(3)
    ]
    total = (
        hidden.astype(jnp.float32) + temporal_bias + prev_ok * taps[0] + taps[1] + next_ok * taps[2]
    )
    return total.astype(jnp.bfloat16)


def solution(mesh):
    frame_n, row_n, col_n = mesh.devices.shape
    fine = Mesh(
        mesh.devices.reshape(frame_n // 2, 2, row_n, col_n // 2, 2),
        ("fy", "fc", "row", "cx", "cz"),
    )
    act = P(FRAME, "row", None, COL)
    weight = P(None, FRAME + ("row",), COL)
    placed = (act, weight, weight, P(COL), P(COL), P())
    return jax.shard_map(body, mesh=fine, in_specs=placed, out_specs=act, check_vma=False)
```

```python
import jax
import jax.numpy as jnp
from jax import lax
from jax.sharding import Mesh
from jax.sharding import PartitionSpec as P

FRAME = ("fy", "fc")
COL = ("cx", "cz")


def shift_halo(block, axis, count, dim, width):
    forward = [(i, i + 1) for i in range(count - 1)]
    backward = [(target, source) for source, target in forward]
    low = lax.ppermute(
        lax.slice_in_dim(block, block.shape[dim] - width, None, axis=dim), axis, forward
    )
    high = lax.ppermute(lax.slice_in_dim(block, 0, width, axis=dim), axis, backward)
    return jnp.concatenate([low, block, high], axis=dim)


def ring_shift(block, axis, count, step):
    return lax.ppermute(block, axis, [(i, (i + step) % count) for i in range(count)])


def col_gather(block):
    width = block.shape[3]
    ring = lax.axis_size("cx")
    me = lax.axis_index("cx")
    side = lax.axis_index("cz")
    partner = lax.ppermute(block, "cz", [(0, 1), (1, 0)])
    pair = jnp.concatenate([block, partner], axis=3)
    from_left = ring_shift(pair, "cx", ring, 1)
    from_right = ring_shift(pair, "cx", ring, -1)
    far_own = ring_shift(from_right[..., :width], "cx", ring, -1)
    far_partner = ring_shift(from_left[..., width:], "cx", ring, 1)
    out = jnp.zeros(block.shape[:3] + (width * 2 * ring,), block.dtype)
    pieces = (
        (0, block, partner),
        (1, from_right[..., :width], from_right[..., width:]),
        (2, far_own, far_partner),
        (ring - 1, from_left[..., :width], from_left[..., width:]),
    )
    for offset, own_side, other_side in pieces:
        place = (me + offset) % ring
        out = lax.dynamic_update_slice_in_dim(out, own_side, (2 * place + side) * width, 3)
        out = lax.dynamic_update_slice_in_dim(out, other_side, (2 * place + 1 - side) * width, 3)
    return out


def weight_gather(weight):
    steps = (("row", 1), ("row", 2), ("row", 4), ("fy", 2), ("fy", 1), ("fc", 1))
    block = weight
    for axis, bit in steps:
        count = lax.axis_size(axis)
        other = lax.ppermute(block, axis, [(i, i ^ bit) for i in range(count)])
        high = (lax.axis_index(axis) // bit) % 2 == 1
        block = jnp.where(high, jnp.stack([other, block]), jnp.stack([block, other]))
    block = jnp.transpose(block, (6, 2, 1, 0, 3, 4, 5, 7, 8))
    taps, depth, width = weight.shape
    return block.reshape(taps, 64 * depth, width)


def spatial_terms(total, gathered, weights):
    row_count = total.shape[1]
    wide = total.shape[2]
    for tap in range(9):
        shift_y, shift_x = (tap // 3, tap % 3)
        window = gathered[:, shift_y : shift_y + row_count, shift_x : shift_x + wide, :]
        total = total + jnp.einsum(
            "fhwc,cd->fhwd", window, weights[tap], preferred_element_type=jnp.float32
        )
    return total


def body(frames_in, spatial_weight, temporal_weight, spatial_bias, temporal_bias, clip_id):
    fr_count, row_count, wide, col_width = frames_in.shape
    both = weight_gather(jnp.concatenate([spatial_weight, temporal_weight], axis=0))
    full_spatial, full_temporal = both[:9], both[9:]
    rimmed = shift_halo(frames_in, "row", lax.axis_size("row"), 1, 1)
    rimmed = jnp.pad(rimmed, ((0, 0), (0, 0), (1, 1), (0, 0)))
    gathered = col_gather(rimmed)
    blank = jnp.zeros((fr_count, row_count, wide, col_width), jnp.float32)
    spatial = spatial_terms(blank, gathered, full_spatial)
    hidden = (spatial + spatial_bias).astype(jnp.bfloat16)
    active = jax.nn.silu(hidden.astype(jnp.float32)).astype(jnp.bfloat16)
    index = lax.axis_index(FRAME)
    edge_ids = jnp.full((1,), -1, jnp.int32)
    padded_ids = jnp.concatenate([edge_ids, clip_id, edge_ids])
    local_ids = lax.dynamic_slice_in_dim(padded_ids, index * fr_count, fr_count + 2)
    prev_ok = (local_ids[1:-1] == local_ids[:-2]).astype(jnp.float32).reshape(fr_count, 1, 1, 1)
    next_ok = (local_ids[1:-1] == local_ids[2:]).astype(jnp.float32).reshape(fr_count, 1, 1, 1)
    source = shift_halo(active, FRAME, lax.axis_size(FRAME), 0, 1)
    whole = col_gather(source)
    taps = [
        jnp.einsum(
            "fhwc,cd->fhwd",
            whole[tap : tap + fr_count],
            full_temporal[tap],
            preferred_element_type=jnp.float32,
        )
        for tap in range(3)
    ]
    total = (
        hidden.astype(jnp.float32) + temporal_bias + prev_ok * taps[0] + taps[1] + next_ok * taps[2]
    )
    return total.astype(jnp.bfloat16)


def solution(mesh):
    frame_n, row_n, col_n = mesh.devices.shape
    fine = Mesh(
        mesh.devices.reshape(frame_n // 2, 2, row_n, col_n // 2, 2),
        ("fy", "fc", "row", "cx", "cz"),
    )
    act = P(FRAME, "row", None, COL)
    weight = P(None, FRAME + ("row",), COL)
    placed = (act, weight, weight, P(COL), P(COL), P())
    return jax.shard_map(body, mesh=fine, in_specs=placed, out_specs=act, check_vma=False)
```

```python
import jax
import jax.numpy as jnp
from jax import lax
from jax.sharding import Mesh
from jax.sharding import PartitionSpec as P

FRAME = ("fy", "fc")
COL = ("cx", "cz")
SWAP = [(0, 1), (1, 0)]


def shift_halo(block, axis, count, dim, width):
    forward = [(i, i + 1) for i in range(count - 1)]
    backward = [(target, source) for source, target in forward]
    low = lax.ppermute(
        lax.slice_in_dim(block, block.shape[dim] - width, None, axis=dim), axis, forward
    )
    high = lax.ppermute(lax.slice_in_dim(block, 0, width, axis=dim), axis, backward)
    return jnp.concatenate([low, block, high], axis=dim)


def ring_shift(block, axis, count, step):
    return lax.ppermute(block, axis, [(i, (i + step) % count) for i in range(count)])


def ordered_pair(own, other, high, dim):
    return jnp.where(
        high, jnp.concatenate([other, own], axis=dim), jnp.concatenate([own, other], axis=dim)
    )


def x_gather(pair, pad):
    ring = lax.axis_size("cx")
    me = lax.axis_index("cx")
    width = pair.shape[3]
    half = width // 2
    from_left = ring_shift(pair, "cx", ring, 1)
    from_right = ring_shift(pair, "cx", ring, -1)
    far_low = ring_shift(from_right[..., :half], "cx", ring, -1)
    far_high = ring_shift(from_left[..., half:], "cx", ring, 1)
    frames, rows, wide, _ = pair.shape
    out = jnp.zeros((frames, rows, wide + 2 * pad, width * ring), pair.dtype)
    pieces = ((0, pair, 0), (1, from_right, 0), (ring - 1, from_left, 0), (2, far_low, 0), (2, far_high, half))
    for offset, piece, shift in pieces:
        base = ((me + offset) % ring) * width + shift
        out = lax.dynamic_update_slice(out, piece, (0, 0, pad, base))
    return out


def weight_gather(weight):
    steps = (("cz", 1), ("row", 4), ("row", 2), ("row", 1), ("fy", 2), ("fy", 1), ("fc", 1))
    block = weight
    for axis, bit in steps:
        count = lax.axis_size(axis)
        other = lax.ppermute(block, axis, [(i, i ^ bit) for i in range(count)])
        high = (lax.axis_index(axis) // bit) % 2 == 1
        block = jnp.where(high, jnp.stack([other, block]), jnp.stack([block, other]))
    block = jnp.transpose(block, (7, 2, 1, 0, 5, 4, 3, 8, 6, 9))
    taps, depth, width = weight.shape
    return block.reshape(taps, 64 * depth, 2 * width)


def spatial_terms(gathered, weights, row_count, wide):
    total = None
    for tap in range(9):
        shift_y, shift_x = (tap // 3, tap % 3)
        window = gathered[:, shift_y : shift_y + row_count, shift_x : shift_x + wide, :]
        term = jnp.einsum("fhwc,cd->fhwd", window, weights[tap], preferred_element_type=jnp.float32)
        total = term if total is None else total + term
    return total


def body(frames_in, spatial_weight, temporal_weight, spatial_bias, temporal_bias, clip_id):
    fr_count, row_count, wide, col_width = frames_in.shape
    half = row_count // 2
    side = lax.axis_index("cz")
    high = side == 1
    both = weight_gather(jnp.concatenate([spatial_weight, temporal_weight], axis=0))
    full_spatial, full_temporal = both[:9], both[9:]
    biases = jnp.stack([spatial_bias, temporal_bias])
    biases = ordered_pair(biases, lax.ppermute(biases, "cz", SWAP), high, 1)
    rimmed = shift_halo(frames_in, "row", lax.axis_size("row"), 1, 1)
    mine = lax.dynamic_slice_in_dim(rimmed, side * half, half + 2, axis=1)
    wanted = lax.dynamic_slice_in_dim(rimmed, (1 - side) * half, half + 2, axis=1)
    partner = lax.ppermute(wanted, "cz", SWAP)
    gathered = x_gather(ordered_pair(mine, partner, high, 3), 1)
    spatial = spatial_terms(gathered, full_spatial, half, wide)
    hidden = (spatial + biases[0]).astype(jnp.bfloat16)
    active = jax.nn.silu(hidden.astype(jnp.float32)).astype(jnp.bfloat16)
    index = lax.axis_index(FRAME)
    edge_ids = jnp.full((1,), -1, jnp.int32)
    padded_ids = jnp.concatenate([edge_ids, clip_id, edge_ids])
    local_ids = lax.dynamic_slice_in_dim(padded_ids, index * fr_count, fr_count + 2)
    prev_ok = (local_ids[1:-1] == local_ids[:-2]).astype(jnp.float32).reshape(fr_count, 1, 1, 1)
    next_ok = (local_ids[1:-1] == local_ids[2:]).astype(jnp.float32).reshape(fr_count, 1, 1, 1)
    source = shift_halo(active, FRAME, lax.axis_size(FRAME), 0, 1)
    whole = x_gather(source, 0)
    taps = [
        jnp.einsum(
            "fhwc,cd->fhwd",
            whole[tap : tap + fr_count],
            full_temporal[tap],
            preferred_element_type=jnp.float32,
        )
        for tap in range(3)
    ]
    total = (
        hidden.astype(jnp.float32) + biases[1] + prev_ok * taps[0] + taps[1] + next_ok * taps[2]
    ).astype(jnp.bfloat16)
    kept = lax.dynamic_slice_in_dim(total, side * col_width, col_width, axis=3)
    given = lax.dynamic_slice_in_dim(total, (1 - side) * col_width, col_width, axis=3)
    returned = lax.ppermute(given, "cz", SWAP)
    return ordered_pair(kept, returned, high, 1)


def solution(mesh):
    frame_n, row_n, col_n = mesh.devices.shape
    fine = Mesh(
        mesh.devices.reshape(frame_n // 2, 2, row_n, col_n // 2, 2),
        ("fy", "fc", "row", "cx", "cz"),
    )
    act = P(FRAME, "row", None, COL)
    weight = P(None, FRAME + ("row",), COL)
    placed = (act, weight, weight, P(COL), P(COL), P())
    return jax.shard_map(body, mesh=fine, in_specs=placed, out_specs=act, check_vma=False)
```

```python
import jax
import jax.numpy as jnp
from jax import lax
from jax.sharding import Mesh
from jax.sharding import PartitionSpec as P

FRAME = ("fy", "fc")
COL = ("cx", "cz")
SWAP = [(0, 1), (1, 0)]


def shift_halo(block, axis, count, dim, width):
    forward = [(i, i + 1) for i in range(count - 1)]
    backward = [(target, source) for source, target in forward]
    low = lax.ppermute(
        lax.slice_in_dim(block, block.shape[dim] - width, None, axis=dim), axis, forward
    )
    high = lax.ppermute(lax.slice_in_dim(block, 0, width, axis=dim), axis, backward)
    return jnp.concatenate([low, block, high], axis=dim)


def ring_shift(block, axis, count, step):
    return lax.ppermute(block, axis, [(i, (i + step) % count) for i in range(count)])


def ordered_pair(own, other, high, dim):
    return jnp.where(
        high, jnp.concatenate([other, own], axis=dim), jnp.concatenate([own, other], axis=dim)
    )


def x_gather(pair):
    ring = lax.axis_size("cx")
    half = pair.shape[3] // 2
    from_left = ring_shift(pair, "cx", ring, 1)
    from_right = ring_shift(pair, "cx", ring, -1)
    far_low = ring_shift(from_right[..., :half], "cx", ring, -1)
    far_high = ring_shift(from_left[..., half:], "cx", ring, 1)
    return jnp.concatenate([pair, from_right, far_low, far_high, from_left], axis=3)


def ring_gather(block, axis):
    ring = lax.axis_size(axis)
    me = lax.axis_index(axis)
    half = block.shape[0] // 2
    from_left = ring_shift(block, axis, ring, 1)
    from_right = ring_shift(block, axis, ring, -1)
    far_low = ring_shift(from_right[:half], axis, ring, -1)
    far_high = ring_shift(from_left[half:], axis, ring, 1)
    far = jnp.concatenate([far_low, far_high], axis=0)
    out = jnp.zeros((ring,) + block.shape, block.dtype)
    for offset, piece in ((0, block), (1, from_right), (2, far), (ring - 1, from_left)):
        start = ((me + offset) % ring,) + (0,) * block.ndim
        out = lax.dynamic_update_slice(out, piece[None], start)
    return out


def swap_stack(block, axis, bit):
    count = lax.axis_size(axis)
    other = lax.ppermute(block, axis, [(i, i ^ bit) for i in range(count)])
    high = (lax.axis_index(axis) // bit) % 2 == 1
    return jnp.where(high, jnp.stack([other, block]), jnp.stack([block, other]))


def weight_gather(weight):
    block = swap_stack(weight, "cz", 1)
    for bit in (4, 2, 1):
        block = swap_stack(block, "row", bit)
    block = ring_gather(block, "fy")
    block = swap_stack(block, "fc", 1)
    block = jnp.transpose(block, (6, 1, 0, 4, 3, 2, 7, 5, 8))
    taps, depth, width = weight.shape
    full = block.reshape(taps, 64 * depth, 2 * width)
    doubled = jnp.concatenate([full, full], axis=1)
    shift = lax.axis_index("cx") * 2 * width
    return lax.dynamic_slice_in_dim(doubled, shift, 64 * depth, axis=1)


def body(frames_in, spatial_weight, temporal_weight, spatial_bias, temporal_bias, clip_id):
    fr_count, row_count, wide, col_width = frames_in.shape
    half = row_count // 2
    side = lax.axis_index("cz")
    high = side == 1
    both = weight_gather(jnp.concatenate([spatial_weight, temporal_weight], axis=0))
    full_spatial, full_temporal = both[:9], both[9:]
    biases = jnp.stack([spatial_bias, temporal_bias])
    biases = ordered_pair(biases, lax.ppermute(biases, "cz", SWAP), high, 1)
    rimmed = shift_halo(frames_in, "row", lax.axis_size("row"), 1, 1)
    mine = lax.dynamic_slice_in_dim(rimmed, side * half, half + 2, axis=1)
    wanted = lax.dynamic_slice_in_dim(rimmed, (1 - side) * half, half + 2, axis=1)
    partner = lax.ppermute(wanted, "cz", SWAP)
    gathered = x_gather(ordered_pair(mine, partner, high, 3))
    kernel = full_spatial.reshape((3, 3) + full_spatial.shape[1:])
    spatial = lax.conv_general_dilated(
        gathered,
        kernel,
        (1, 1),
        ((0, 0), (1, 1)),
        dimension_numbers=("NHWC", "HWIO", "NHWC"),
        preferred_element_type=jnp.float32,
    )
    hidden = (spatial + biases[0]).astype(jnp.bfloat16)
    active = jax.nn.silu(hidden.astype(jnp.float32)).astype(jnp.bfloat16)
    index = lax.axis_index(FRAME)
    edge_ids = jnp.full((1,), -1, jnp.int32)
    padded_ids = jnp.concatenate([edge_ids, clip_id, edge_ids])
    local_ids = lax.dynamic_slice_in_dim(padded_ids, index * fr_count, fr_count + 2)
    prev_ok = (local_ids[1:-1] == local_ids[:-2]).astype(jnp.float32).reshape(fr_count, 1, 1, 1)
    next_ok = (local_ids[1:-1] == local_ids[2:]).astype(jnp.float32).reshape(fr_count, 1, 1, 1)
    source = shift_halo(active, FRAME, lax.axis_size(FRAME), 0, 1)
    whole = x_gather(source)
    taps = [
        jnp.einsum(
            "fhwc,cd->fhwd",
            whole[tap : tap + fr_count],
            full_temporal[tap],
            preferred_element_type=jnp.float32,
        )
        for tap in range(3)
    ]
    total = (
        hidden.astype(jnp.float32) + biases[1] + prev_ok * taps[0] + taps[1] + next_ok * taps[2]
    ).astype(jnp.bfloat16)
    kept = lax.dynamic_slice_in_dim(total, side * col_width, col_width, axis=3)
    given = lax.dynamic_slice_in_dim(total, (1 - side) * col_width, col_width, axis=3)
    returned = lax.ppermute(given, "cz", SWAP)
    return ordered_pair(kept, returned, high, 1)


def solution(mesh):
    frame_n, row_n, col_n = mesh.devices.shape
    fine = Mesh(
        mesh.devices.reshape(frame_n // 2, 2, row_n, col_n // 2, 2),
        ("fy", "fc", "row", "cx", "cz"),
    )
    act = P(FRAME, "row", None, COL)
    weight = P(None, FRAME + ("row",), COL)
    placed = (act, weight, weight, P(COL), P(COL), P())
    return jax.shard_map(body, mesh=fine, in_specs=placed, out_specs=act, check_vma=False)
```

```python
import jax
import jax.numpy as jnp
from jax import lax
from jax.sharding import Mesh
from jax.sharding import PartitionSpec as P

FRAME = ("fy", "fc")
COL = ("cx", "cz")
SWAP = [(0, 1), (1, 0)]


def shift_halo(block, axis, count, dim, width):
    forward = [(i, i + 1) for i in range(count - 1)]
    backward = [(target, source) for source, target in forward]
    low = lax.ppermute(
        lax.slice_in_dim(block, block.shape[dim] - width, None, axis=dim), axis, forward
    )
    high = lax.ppermute(lax.slice_in_dim(block, 0, width, axis=dim), axis, backward)
    return jnp.concatenate([low, block, high], axis=dim)


def ring_shift(block, axis, count, step):
    return lax.ppermute(block, axis, [(i, (i + step) % count) for i in range(count)])


def ordered_pair(own, other, high, dim):
    return jnp.where(
        high, jnp.concatenate([other, own], axis=dim), jnp.concatenate([own, other], axis=dim)
    )


def x_gather(pair):
    ring = lax.axis_size("cx")
    half = pair.shape[3] // 2
    from_left = ring_shift(pair, "cx", ring, 1)
    from_right = ring_shift(pair, "cx", ring, -1)
    far_low = ring_shift(from_right[..., :half], "cx", ring, -1)
    far_high = ring_shift(from_left[..., half:], "cx", ring, 1)
    return jnp.concatenate([pair, from_right, far_low, far_high, from_left], axis=3)


def ring_gather(block, axis, dim, rotate):
    ring = lax.axis_size(axis)
    me = lax.axis_index(axis)
    half = block.shape[dim] // 2
    from_left = ring_shift(block, axis, ring, 1)
    from_right = ring_shift(block, axis, ring, -1)
    far_low = ring_shift(lax.slice_in_dim(from_right, 0, half, axis=dim), axis, ring, -1)
    far_high = ring_shift(lax.slice_in_dim(from_left, half, None, axis=dim), axis, ring, 1)
    far = jnp.concatenate([far_low, far_high], axis=dim)
    shape = block.shape[:dim] + (ring,) + block.shape[dim:]
    out = jnp.zeros(shape, block.dtype)
    for offset, piece in ((0, block), (1, from_right), (2, far), (ring - 1, from_left)):
        start = [0] * len(shape)
        start[dim] = (me + offset - rotate + 2 * ring) % ring
        out = lax.dynamic_update_slice(out, jnp.expand_dims(piece, dim), start)
    return out


def weight_gather(weight):
    taps, depth, width = weight.shape
    high_z = lax.axis_index("cz") == 1
    block = ordered_pair(weight, lax.ppermute(weight, "cz", SWAP), high_z, 2)
    row_n = lax.axis_size("row")
    for pos, bit in enumerate((4, 2, 1)):
        other = lax.ppermute(block, "row", [(i, i ^ bit) for i in range(row_n)])
        high = (lax.axis_index("row") // bit) % 2 == 1
        block = jnp.where(
            high, jnp.stack([other, block], axis=1 + pos), jnp.stack([block, other], axis=1 + pos)
        )
    block = block.reshape(taps, row_n * depth, 2 * width)
    block = ring_gather(block, "fy", 1, lax.axis_index("cx"))
    high_c = lax.axis_index("fc") == 1
    other = lax.ppermute(block, "fc", SWAP)
    block = jnp.where(high_c, jnp.stack([other, block], axis=2), jnp.stack([block, other], axis=2))
    return block.reshape(taps, -1, 2 * width)


def body(frames_in, spatial_weight, temporal_weight, spatial_bias, temporal_bias, clip_id):
    fr_count, row_count, wide, col_width = frames_in.shape
    half = row_count // 2
    side = lax.axis_index("cz")
    high = side == 1
    both = weight_gather(jnp.concatenate([spatial_weight, temporal_weight], axis=0))
    full_spatial, full_temporal = both[:9], both[9:]
    biases = jnp.stack([spatial_bias, temporal_bias])
    biases = ordered_pair(biases, lax.ppermute(biases, "cz", SWAP), high, 1)
    rimmed = shift_halo(frames_in, "row", lax.axis_size("row"), 1, 1)
    mine = lax.dynamic_slice_in_dim(rimmed, side * half, half + 2, axis=1)
    wanted = lax.dynamic_slice_in_dim(rimmed, (1 - side) * half, half + 2, axis=1)
    partner = lax.ppermute(wanted, "cz", SWAP)
    gathered = x_gather(ordered_pair(mine, partner, high, 3))
    kernel = full_spatial.reshape((3, 3) + full_spatial.shape[1:])
    spatial = lax.conv_general_dilated(
        gathered,
        kernel,
        (1, 1),
        ((0, 0), (1, 1)),
        dimension_numbers=("NHWC", "HWIO", "NHWC"),
        preferred_element_type=jnp.float32,
    )
    hidden = (spatial + biases[0]).astype(jnp.bfloat16)
    active = jax.nn.silu(hidden.astype(jnp.float32)).astype(jnp.bfloat16)
    index = lax.axis_index(FRAME)
    edge_ids = jnp.full((1,), -1, jnp.int32)
    padded_ids = jnp.concatenate([edge_ids, clip_id, edge_ids])
    local_ids = lax.dynamic_slice_in_dim(padded_ids, index * fr_count, fr_count + 2)
    prev_ok = (local_ids[1:-1] == local_ids[:-2]).astype(jnp.float32).reshape(fr_count, 1, 1, 1)
    next_ok = (local_ids[1:-1] == local_ids[2:]).astype(jnp.float32).reshape(fr_count, 1, 1, 1)
    source = shift_halo(active, FRAME, lax.axis_size(FRAME), 0, 1)
    whole = x_gather(source)
    taps = [
        jnp.einsum(
            "fhwc,cd->fhwd",
            whole[tap : tap + fr_count],
            full_temporal[tap],
            preferred_element_type=jnp.float32,
        )
        for tap in range(3)
    ]
    total = (
        hidden.astype(jnp.float32) + biases[1] + prev_ok * taps[0] + taps[1] + next_ok * taps[2]
    ).astype(jnp.bfloat16)
    kept = lax.dynamic_slice_in_dim(total, side * col_width, col_width, axis=3)
    given = lax.dynamic_slice_in_dim(total, (1 - side) * col_width, col_width, axis=3)
    returned = lax.ppermute(given, "cz", SWAP)
    return ordered_pair(kept, returned, high, 1)


def solution(mesh):
    frame_n, row_n, col_n = mesh.devices.shape
    fine = Mesh(
        mesh.devices.reshape(frame_n // 2, 2, row_n, col_n // 2, 2),
        ("fy", "fc", "row", "cx", "cz"),
    )
    act = P(FRAME, "row", None, COL)
    weight = P(None, FRAME + ("row",), COL)
    placed = (act, weight, weight, P(COL), P(COL), P())
    return jax.shard_map(body, mesh=fine, in_specs=placed, out_specs=act, check_vma=False)
```

```python
import jax
import jax.numpy as jnp
from jax import lax
from jax.sharding import Mesh
from jax.sharding import PartitionSpec as P

FRAME = ("fy", "fc")
COL = ("cx", "cz")
SWAP = [(0, 1), (1, 0)]


def shift_halo(block, axis, count, dim, width):
    forward = [(i, i + 1) for i in range(count - 1)]
    backward = [(target, source) for source, target in forward]
    low = lax.ppermute(
        lax.slice_in_dim(block, block.shape[dim] - width, None, axis=dim), axis, forward
    )
    high = lax.ppermute(lax.slice_in_dim(block, 0, width, axis=dim), axis, backward)
    return jnp.concatenate([low, block, high], axis=dim)


def ring_shift(block, axis, count, step):
    return lax.ppermute(block, axis, [(i, (i + step) % count) for i in range(count)])


def ordered_pair(own, other, high, dim):
    return jnp.where(
        high, jnp.concatenate([other, own], axis=dim), jnp.concatenate([own, other], axis=dim)
    )


def x_gather(pair):
    ring = lax.axis_size("cx")
    half = pair.shape[3] // 2
    from_left = ring_shift(pair, "cx", ring, 1)
    from_right = ring_shift(pair, "cx", ring, -1)
    far_low = ring_shift(from_right[..., :half], "cx", ring, -1)
    far_high = ring_shift(from_left[..., half:], "cx", ring, 1)
    return jnp.concatenate([pair, from_right, far_low, far_high, from_left], axis=3)


def xor_stack(block, axis, bit, pos):
    count = lax.axis_size(axis)
    other = lax.ppermute(block, axis, [(i, i ^ bit) for i in range(count)])
    high = (lax.axis_index(axis) // bit) % 2 == 1
    return jnp.where(high, jnp.stack([other, block], axis=pos), jnp.stack([block, other], axis=pos))


def body(frames_in, spatial_weight, temporal_weight, spatial_bias, temporal_bias, clip_id):
    fr_count, row_count, wide, col_width = frames_in.shape
    half = row_count // 2
    side = lax.axis_index("cz")
    high = side == 1
    row_n = lax.axis_size("row")
    ring = lax.axis_size("cx")
    weight = jnp.concatenate([spatial_weight, temporal_weight], axis=0)
    taps, depth, _ = weight.shape
    biases = jnp.stack([spatial_bias, temporal_bias])
    biases = ordered_pair(biases, lax.ppermute(biases, "cz", SWAP), high, 1)
    rimmed = shift_halo(frames_in, "row", row_n, 1, 1)
    w_block = ordered_pair(weight, lax.ppermute(weight, "cz", SWAP), high, 2)
    rimmed, w_block = lax.optimization_barrier((rimmed, w_block))
    mine = lax.dynamic_slice_in_dim(rimmed, side * half, half + 2, axis=1)
    wanted = lax.dynamic_slice_in_dim(rimmed, (1 - side) * half, half + 2, axis=1)
    partner = lax.ppermute(wanted, "cz", SWAP)
    for pos, bit in enumerate((4, 2, 1)):
        w_block = xor_stack(w_block, "row", bit, 1 + pos)
    w_block = w_block.reshape(taps, row_n * depth, -1)
    partner, w_block = lax.optimization_barrier((partner, w_block))
    pair = ordered_pair(mine, partner, high, 3)
    from_left = ring_shift(pair, "cx", ring, 1)
    from_right = ring_shift(pair, "cx", ring, -1)
    fy_n = lax.axis_size("fy")
    w_left = ring_shift(w_block, "fy", fy_n, 1)
    w_right = ring_shift(w_block, "fy", fy_n, -1)
    from_left, from_right, w_left, w_right = lax.optimization_barrier(
        (from_left, from_right, w_left, w_right)
    )
    cut = pair.shape[3] // 2
    far_low = ring_shift(from_right[..., :cut], "cx", ring, -1)
    far_high = ring_shift(from_left[..., cut:], "cx", ring, 1)
    w_cut = w_block.shape[1] // 2
    w_far_low = ring_shift(w_right[:, :w_cut], "fy", fy_n, -1)
    w_far_high = ring_shift(w_left[:, w_cut:], "fy", fy_n, 1)
    far_low, far_high, w_far_low, w_far_high = lax.optimization_barrier(
        (far_low, far_high, w_far_low, w_far_high)
    )
    gathered = jnp.concatenate([pair, from_right, far_low, far_high, from_left], axis=3)
    me_fy = lax.axis_index("fy")
    rotate = lax.axis_index("cx")
    w_far = jnp.concatenate([w_far_low, w_far_high], axis=1)
    w_out = jnp.zeros((taps, fy_n) + w_block.shape[1:], w_block.dtype)
    for offset, piece in ((0, w_block), (1, w_right), (2, w_far), (fy_n - 1, w_left)):
        place = (me_fy + offset - rotate + 2 * fy_n) % fy_n
        w_out = lax.dynamic_update_slice(w_out, piece[:, None], (0, place, 0, 0))
    both = xor_stack(w_out, "fc", 1, 2).reshape(taps, -1, w_block.shape[2])
    full_spatial, full_temporal = both[:9], both[9:]
    kernel = full_spatial.reshape((3, 3) + full_spatial.shape[1:])
    spatial = lax.conv_general_dilated(
        gathered,
        kernel,
        (1, 1),
        ((0, 0), (1, 1)),
        dimension_numbers=("NHWC", "HWIO", "NHWC"),
        preferred_element_type=jnp.float32,
    )
    hidden = (spatial + biases[0]).astype(jnp.bfloat16)
    active = jax.nn.silu(hidden.astype(jnp.float32)).astype(jnp.bfloat16)
    index = lax.axis_index(FRAME)
    edge_ids = jnp.full((1,), -1, jnp.int32)
    padded_ids = jnp.concatenate([edge_ids, clip_id, edge_ids])
    local_ids = lax.dynamic_slice_in_dim(padded_ids, index * fr_count, fr_count + 2)
    prev_ok = (local_ids[1:-1] == local_ids[:-2]).astype(jnp.float32).reshape(fr_count, 1, 1, 1)
    next_ok = (local_ids[1:-1] == local_ids[2:]).astype(jnp.float32).reshape(fr_count, 1, 1, 1)
    source = shift_halo(active, FRAME, lax.axis_size(FRAME), 0, 1)
    whole = x_gather(source)
    taps_out = [
        jnp.einsum(
            "fhwc,cd->fhwd",
            whole[tap : tap + fr_count],
            full_temporal[tap],
            preferred_element_type=jnp.float32,
        )
        for tap in range(3)
    ]
    total = (
        hidden.astype(jnp.float32)
        + biases[1]
        + prev_ok * taps_out[0]
        + taps_out[1]
        + next_ok * taps_out[2]
    ).astype(jnp.bfloat16)
    kept = lax.dynamic_slice_in_dim(total, side * col_width, col_width, axis=3)
    given = lax.dynamic_slice_in_dim(total, (1 - side) * col_width, col_width, axis=3)
    returned = lax.ppermute(given, "cz", SWAP)
    return ordered_pair(kept, returned, high, 1)


def solution(mesh):
    frame_n, row_n, col_n = mesh.devices.shape
    fine = Mesh(
        mesh.devices.reshape(frame_n // 2, 2, row_n, col_n // 2, 2),
        ("fy", "fc", "row", "cx", "cz"),
    )
    act = P(FRAME, "row", None, COL)
    weight = P(None, FRAME + ("row",), COL)
    placed = (act, weight, weight, P(COL), P(COL), P())
    return jax.shard_map(body, mesh=fine, in_specs=placed, out_specs=act, check_vma=False)
```

```python
import jax
import jax.numpy as jnp
from jax import lax
from jax.sharding import Mesh
from jax.sharding import PartitionSpec as P

FRAME = ("fy", "fc")
COL = ("cx", "cz")
SWAP = [(0, 1), (1, 0)]


def shift_halo(block, axis, count, dim, width):
    forward = [(i, i + 1) for i in range(count - 1)]
    backward = [(target, source) for source, target in forward]
    low = lax.ppermute(
        lax.slice_in_dim(block, block.shape[dim] - width, None, axis=dim), axis, forward
    )
    high = lax.ppermute(lax.slice_in_dim(block, 0, width, axis=dim), axis, backward)
    return jnp.concatenate([low, block, high], axis=dim)


def ring_shift(block, axis, count, step):
    return lax.ppermute(block, axis, [(i, (i + step) % count) for i in range(count)])


def ordered_pair(own, other, high, dim):
    return jnp.where(
        high, jnp.concatenate([other, own], axis=dim), jnp.concatenate([own, other], axis=dim)
    )


def x_gather(pair):
    ring = lax.axis_size("cx")
    half = pair.shape[3] // 2
    from_left = ring_shift(pair, "cx", ring, 1)
    from_right = ring_shift(pair, "cx", ring, -1)
    far_low = ring_shift(from_right[..., :half], "cx", ring, -1)
    far_high = ring_shift(from_left[..., half:], "cx", ring, 1)
    return jnp.concatenate([pair, from_right, far_low, far_high, from_left], axis=3)


def xor_stack(block, axis, bit, pos):
    count = lax.axis_size(axis)
    other = lax.ppermute(block, axis, [(i, i ^ bit) for i in range(count)])
    high = (lax.axis_index(axis) // bit) % 2 == 1
    return jnp.where(high, jnp.stack([other, block], axis=pos), jnp.stack([block, other], axis=pos))


def body(frames_in, spatial_weight, temporal_weight, spatial_bias, temporal_bias, clip_id):
    fr_count, row_count, wide, col_width = frames_in.shape
    half = row_count // 2
    side = lax.axis_index("cz")
    high = side == 1
    row_n = lax.axis_size("row")
    ring = lax.axis_size("cx")
    weight = jnp.concatenate([spatial_weight, temporal_weight], axis=0)
    taps, depth, _ = weight.shape
    biases = jnp.stack([spatial_bias, temporal_bias])
    biases = ordered_pair(biases, lax.ppermute(biases, "cz", SWAP), high, 1)
    rimmed = shift_halo(frames_in, "row", row_n, 1, 1)
    sent = lax.dynamic_slice_in_dim(frames_in, (1 - side) * (half - 1), half + 1, axis=1)
    partner = lax.ppermute(sent, "cz", SWAP)
    edge = lax.dynamic_slice_in_dim(frames_in, side * (row_count - 1), 1, axis=1)
    diagonal = [(q * 2 + 1, q * 2 + 2) for q in range(row_n - 1)]
    diagonal += [(q * 2, q * 2 - 1) for q in range(1, row_n)]
    rim = lax.ppermute(edge, ("row", "cz"), diagonal)
    w_block = ordered_pair(weight, lax.ppermute(weight, "cz", SWAP), high, 2)
    rimmed, w_block = lax.optimization_barrier((rimmed, w_block))
    mine = lax.dynamic_slice_in_dim(rimmed, side * half, half + 2, axis=1)
    own_left = ring_shift(mine, "cx", ring, 1)
    own_right = ring_shift(mine, "cx", ring, -1)
    for pos, bit in enumerate((4, 2, 1)):
        w_block = xor_stack(w_block, "row", bit, 1 + pos)
    w_block = w_block.reshape(taps, row_n * depth, -1)
    own_left, own_right, w_block, partner, rim = lax.optimization_barrier(
        (own_left, own_right, w_block, partner, rim)
    )
    other = ordered_pair(rim, partner, high, 1)
    other_left = ring_shift(other, "cx", ring, 1)
    other_right = ring_shift(other, "cx", ring, -1)
    far_own = ring_shift(own_right, "cx", ring, -1)
    fy_n = lax.axis_size("fy")
    w_left = ring_shift(w_block, "fy", fy_n, 1)
    w_right = ring_shift(w_block, "fy", fy_n, -1)
    other_left, other_right, far_own, w_left, w_right = lax.optimization_barrier(
        (other_left, other_right, far_own, w_left, w_right)
    )
    far_other = ring_shift(other_left, "cx", ring, 1)
    w_cut = w_block.shape[1] // 2
    w_far_low = ring_shift(w_right[:, :w_cut], "fy", fy_n, -1)
    w_far_high = ring_shift(w_left[:, w_cut:], "fy", fy_n, 1)
    far_other, w_far_low, w_far_high = lax.optimization_barrier((far_other, w_far_low, w_far_high))
    gathered = jnp.concatenate(
        [mine, other, own_right, other_right, far_own, far_other, own_left, other_left], axis=3
    )
    me_fy = lax.axis_index("fy")
    rotate = lax.axis_index("cx")
    w_far = jnp.concatenate([w_far_low, w_far_high], axis=1)
    w_out = jnp.zeros((taps, fy_n) + w_block.shape[1:], w_block.dtype)
    for offset, piece in ((0, w_block), (1, w_right), (2, w_far), (fy_n - 1, w_left)):
        place = (me_fy + offset - rotate + 2 * fy_n) % fy_n
        w_out = lax.dynamic_update_slice(w_out, piece[:, None], (0, place, 0, 0))
    w_other = lax.ppermute(w_out, "fc", SWAP)
    flip = (lax.axis_index("fc") + side) % 2 == 1
    both = jnp.where(flip, jnp.stack([w_other, w_out], axis=2), jnp.stack([w_out, w_other], axis=2))
    both = both.reshape(taps, -1, w_block.shape[2])
    full_spatial, full_temporal = both[:9], both[9:]
    kernel = full_spatial.reshape((3, 3) + full_spatial.shape[1:])
    spatial = lax.conv_general_dilated(
        gathered,
        kernel,
        (1, 1),
        ((0, 0), (1, 1)),
        dimension_numbers=("NHWC", "HWIO", "NHWC"),
        preferred_element_type=jnp.float32,
    )
    hidden = (spatial + biases[0]).astype(jnp.bfloat16)
    active = jax.nn.silu(hidden.astype(jnp.float32)).astype(jnp.bfloat16)
    index = lax.axis_index(FRAME)
    edge_ids = jnp.full((1,), -1, jnp.int32)
    padded_ids = jnp.concatenate([edge_ids, clip_id, edge_ids])
    local_ids = lax.dynamic_slice_in_dim(padded_ids, index * fr_count, fr_count + 2)
    prev_ok = (local_ids[1:-1] == local_ids[:-2]).astype(jnp.float32).reshape(fr_count, 1, 1, 1)
    next_ok = (local_ids[1:-1] == local_ids[2:]).astype(jnp.float32).reshape(fr_count, 1, 1, 1)
    source = shift_halo(active, FRAME, lax.axis_size(FRAME), 0, 1)
    source = jnp.where(
        high, jnp.concatenate([source[..., col_width:], source[..., :col_width]], axis=3), source
    )
    whole = x_gather(source)
    taps_out = [
        jnp.einsum(
            "fhwc,cd->fhwd",
            whole[tap : tap + fr_count],
            full_temporal[tap],
            preferred_element_type=jnp.float32,
        )
        for tap in range(3)
    ]
    total = (
        hidden.astype(jnp.float32)
        + biases[1]
        + prev_ok * taps_out[0]
        + taps_out[1]
        + next_ok * taps_out[2]
    ).astype(jnp.bfloat16)
    kept = lax.dynamic_slice_in_dim(total, side * col_width, col_width, axis=3)
    given = lax.dynamic_slice_in_dim(total, (1 - side) * col_width, col_width, axis=3)
    returned = lax.ppermute(given, "cz", SWAP)
    return ordered_pair(kept, returned, high, 1)


def solution(mesh):
    frame_n, row_n, col_n = mesh.devices.shape
    fine = Mesh(
        mesh.devices.reshape(frame_n // 2, 2, row_n, col_n // 2, 2),
        ("fy", "fc", "row", "cx", "cz"),
    )
    act = P(FRAME, "row", None, COL)
    weight = P(None, FRAME + ("row",), COL)
    placed = (act, weight, weight, P(COL), P(COL), P())
    return jax.shard_map(body, mesh=fine, in_specs=placed, out_specs=act, check_vma=False)
```

```python
import jax
import jax.numpy as jnp
from jax import lax
from jax.sharding import Mesh
from jax.sharding import PartitionSpec as P

FRAME = ("fy", "fc")
COL = ("cx", "cz")
SWAP = [(0, 1), (1, 0)]


def shift_halo(block, axis, count, dim, width):
    forward = [(i, i + 1) for i in range(count - 1)]
    backward = [(target, source) for source, target in forward]
    low = lax.ppermute(
        lax.slice_in_dim(block, block.shape[dim] - width, None, axis=dim), axis, forward
    )
    high = lax.ppermute(lax.slice_in_dim(block, 0, width, axis=dim), axis, backward)
    return jnp.concatenate([low, block, high], axis=dim)


def ring_shift(block, axis, count, step):
    return lax.ppermute(block, axis, [(i, (i + step) % count) for i in range(count)])


def ordered_pair(own, other, high, dim):
    return jnp.where(
        high, jnp.concatenate([other, own], axis=dim), jnp.concatenate([own, other], axis=dim)
    )


def x_gather(pair):
    ring = lax.axis_size("cx")
    half = pair.shape[3] // 2
    from_left = ring_shift(pair, "cx", ring, 1)
    from_right = ring_shift(pair, "cx", ring, -1)
    far_low = ring_shift(from_right[..., :half], "cx", ring, -1)
    far_high = ring_shift(from_left[..., half:], "cx", ring, 1)
    return jnp.concatenate([pair, from_right, far_low, far_high, from_left], axis=3)


def xor_stack(block, axis, bit, pos):
    count = lax.axis_size(axis)
    other = lax.ppermute(block, axis, [(i, i ^ bit) for i in range(count)])
    high = (lax.axis_index(axis) // bit) % 2 == 1
    return jnp.where(high, jnp.stack([other, block], axis=pos), jnp.stack([block, other], axis=pos))


def body(frames_in, spatial_weight, temporal_weight, spatial_bias, temporal_bias, clip_id):
    fr_count, row_count, wide, col_width = frames_in.shape
    half = row_count // 2
    side = lax.axis_index("cz")
    high = side == 1
    row_n = lax.axis_size("row")
    ring = lax.axis_size("cx")
    weight = jnp.concatenate([spatial_weight, temporal_weight], axis=0)
    taps, depth, _ = weight.shape
    biases = jnp.stack([spatial_bias, temporal_bias])
    biases = ordered_pair(biases, lax.ppermute(biases, "cz", SWAP), high, 1)
    rimmed = shift_halo(frames_in, "row", row_n, 1, 1)
    sent = lax.dynamic_slice_in_dim(frames_in, (1 - side) * (half - 1), half + 1, axis=1)
    partner = lax.ppermute(sent, "cz", SWAP)
    edge = lax.dynamic_slice_in_dim(frames_in, side * (row_count - 1), 1, axis=1)
    diagonal = [(q * 2 + 1, q * 2 + 2) for q in range(row_n - 1)]
    diagonal += [(q * 2, q * 2 - 1) for q in range(1, row_n)]
    rim = lax.ppermute(edge, ("row", "cz"), diagonal)
    w_block = ordered_pair(weight, lax.ppermute(weight, "cz", SWAP), high, 2)
    rimmed, partner, rim, w_block = lax.optimization_barrier((rimmed, partner, rim, w_block))
    mine = lax.dynamic_slice_in_dim(rimmed, side * half, half + 2, axis=1)
    pair = ordered_pair(mine, ordered_pair(rim, partner, high, 1), high, 3)
    from_left = ring_shift(pair, "cx", ring, 1)
    from_right = ring_shift(pair, "cx", ring, -1)
    for pos, bit in enumerate((4, 2, 1)):
        w_block = xor_stack(w_block, "row", bit, 1 + pos)
    w_block = w_block.reshape(taps, row_n * depth, -1)
    from_left, from_right, w_block = lax.optimization_barrier((from_left, from_right, w_block))
    fy_n = lax.axis_size("fy")
    w_left = ring_shift(w_block, "fy", fy_n, 1)
    w_right = ring_shift(w_block, "fy", fy_n, -1)
    cut = pair.shape[3] // 2
    far_low = ring_shift(from_right[..., :cut], "cx", ring, -1)
    far_high = ring_shift(from_left[..., cut:], "cx", ring, 1)
    far_low, far_high, w_left, w_right = lax.optimization_barrier((far_low, far_high, w_left, w_right))
    w_cut = w_block.shape[1] // 2
    w_far_low = ring_shift(w_right[:, :w_cut], "fy", fy_n, -1)
    w_far_high = ring_shift(w_left[:, w_cut:], "fy", fy_n, 1)
    gathered = jnp.concatenate([pair, from_right, far_low, far_high, from_left], axis=3)
    me_fy = lax.axis_index("fy")
    rotate = lax.axis_index("cx")
    w_far = jnp.concatenate([w_far_low, w_far_high], axis=1)
    w_out = jnp.zeros((taps, fy_n) + w_block.shape[1:], w_block.dtype)
    for offset, piece in ((0, w_block), (1, w_right), (2, w_far), (fy_n - 1, w_left)):
        place = (me_fy + offset - rotate + 2 * fy_n) % fy_n
        w_out = lax.dynamic_update_slice(w_out, piece[:, None], (0, place, 0, 0))
    both = xor_stack(w_out, "fc", 1, 2).reshape(taps, -1, w_block.shape[2])
    full_spatial, full_temporal = both[:9], both[9:]
    kernel = full_spatial.reshape((3, 3) + full_spatial.shape[1:])
    spatial = lax.conv_general_dilated(
        gathered,
        kernel,
        (1, 1),
        ((0, 0), (1, 1)),
        dimension_numbers=("NHWC", "HWIO", "NHWC"),
        preferred_element_type=jnp.float32,
    )
    hidden = (spatial + biases[0]).astype(jnp.bfloat16)
    active = jax.nn.silu(hidden.astype(jnp.float32)).astype(jnp.bfloat16)
    index = lax.axis_index(FRAME)
    edge_ids = jnp.full((1,), -1, jnp.int32)
    padded_ids = jnp.concatenate([edge_ids, clip_id, edge_ids])
    local_ids = lax.dynamic_slice_in_dim(padded_ids, index * fr_count, fr_count + 2)
    prev_ok = (local_ids[1:-1] == local_ids[:-2]).astype(jnp.float32).reshape(fr_count, 1, 1, 1)
    next_ok = (local_ids[1:-1] == local_ids[2:]).astype(jnp.float32).reshape(fr_count, 1, 1, 1)
    source = shift_halo(active, FRAME, lax.axis_size(FRAME), 0, 1)
    whole = x_gather(source)
    taps_out = [
        jnp.einsum(
            "fhwc,cd->fhwd",
            whole[tap : tap + fr_count],
            full_temporal[tap],
            preferred_element_type=jnp.float32,
        )
        for tap in range(3)
    ]
    total = (
        hidden.astype(jnp.float32)
        + biases[1]
        + prev_ok * taps_out[0]
        + taps_out[1]
        + next_ok * taps_out[2]
    ).astype(jnp.bfloat16)
    kept = lax.dynamic_slice_in_dim(total, side * col_width, col_width, axis=3)
    given = lax.dynamic_slice_in_dim(total, (1 - side) * col_width, col_width, axis=3)
    returned = lax.ppermute(given, "cz", SWAP)
    return ordered_pair(kept, returned, high, 1)


def solution(mesh):
    frame_n, row_n, col_n = mesh.devices.shape
    fine = Mesh(
        mesh.devices.reshape(frame_n // 2, 2, row_n, col_n // 2, 2),
        ("fy", "fc", "row", "cx", "cz"),
    )
    act = P(FRAME, "row", None, COL)
    weight = P(None, FRAME + ("row",), COL)
    placed = (act, weight, weight, P(COL), P(COL), P())
    return jax.shard_map(body, mesh=fine, in_specs=placed, out_specs=act, check_vma=False)
```

```python
import jax
import jax.numpy as jnp
from jax import lax
from jax.sharding import Mesh
from jax.sharding import PartitionSpec as P

FRAME = ("fy", "fc")
COL = ("cx", "cz")
SWAP = [(0, 1), (1, 0)]


def shift_halo(block, axis, count, dim, width):
    forward = [(i, i + 1) for i in range(count - 1)]
    backward = [(target, source) for source, target in forward]
    low = lax.ppermute(
        lax.slice_in_dim(block, block.shape[dim] - width, None, axis=dim), axis, forward
    )
    high = lax.ppermute(lax.slice_in_dim(block, 0, width, axis=dim), axis, backward)
    return jnp.concatenate([low, block, high], axis=dim)


def ring_shift(block, axis, count, step):
    return lax.ppermute(block, axis, [(i, (i + step) % count) for i in range(count)])


def ordered_pair(own, other, high, dim):
    return jnp.where(
        high, jnp.concatenate([other, own], axis=dim), jnp.concatenate([own, other], axis=dim)
    )


def x_gather(pair):
    ring = lax.axis_size("cx")
    half = pair.shape[3] // 2
    from_left = ring_shift(pair, "cx", ring, 1)
    from_right = ring_shift(pair, "cx", ring, -1)
    far_low = ring_shift(from_right[..., :half], "cx", ring, -1)
    far_high = ring_shift(from_left[..., half:], "cx", ring, 1)
    return jnp.concatenate([pair, from_right, far_low, far_high, from_left], axis=3)


def xor_stack(block, axis, bit, pos):
    count = lax.axis_size(axis)
    other = lax.ppermute(block, axis, [(i, i ^ bit) for i in range(count)])
    high = (lax.axis_index(axis) // bit) % 2 == 1
    return jnp.where(high, jnp.stack([other, block], axis=pos), jnp.stack([block, other], axis=pos))


def body(frames_in, spatial_weight, temporal_weight, spatial_bias, temporal_bias, clip_id):
    fr_count, row_count, wide, col_width = frames_in.shape
    half = row_count // 2
    side = lax.axis_index("cz")
    high = side == 1
    row_n = lax.axis_size("row")
    ring = lax.axis_size("cx")
    weight = jnp.concatenate([spatial_weight, temporal_weight], axis=0)
    taps, depth, _ = weight.shape
    biases = jnp.stack([spatial_bias, temporal_bias])
    biases = ordered_pair(biases, lax.ppermute(biases, "cz", SWAP), high, 1)
    rimmed = shift_halo(frames_in, "row", row_n, 1, 1)
    sent = lax.dynamic_slice_in_dim(frames_in, (1 - side) * (half - 1), half + 1, axis=1)
    partner = lax.ppermute(sent, "cz", SWAP)
    edge = lax.dynamic_slice_in_dim(frames_in, side * (row_count - 1), 1, axis=1)
    diagonal = [(q * 2 + 1, q * 2 + 2) for q in range(row_n - 1)]
    diagonal += [(q * 2, q * 2 - 1) for q in range(1, row_n)]
    rim = lax.ppermute(edge, ("row", "cz"), diagonal)
    w_block = ordered_pair(weight, lax.ppermute(weight, "cz", SWAP), high, 2)
    rimmed, partner, rim, w_block = lax.optimization_barrier((rimmed, partner, rim, w_block))
    mine = lax.dynamic_slice_in_dim(rimmed, side * half, half + 2, axis=1)
    pair = ordered_pair(mine, ordered_pair(rim, partner, high, 1), high, 3)
    from_left = ring_shift(pair, "cx", ring, 1)
    from_right = ring_shift(pair, "cx", ring, -1)
    w_block = xor_stack(w_block, "row", row_n // 2, 1)
    low_n = row_n // 2
    low = lax.axis_index("row") % low_n
    w_group = jnp.zeros((taps, 2, low_n) + w_block.shape[2:], w_block.dtype)
    for flip in range(low_n):
        if flip == 0:
            piece = w_block
        else:
            piece = lax.ppermute(w_block, "row", [(i, i ^ flip) for i in range(row_n)])
        w_group = lax.dynamic_update_slice(w_group, piece[:, :, None], (0, 0, low ^ flip, 0, 0))
    w_block = w_group.reshape(taps, row_n * depth, -1)
    from_left, from_right, w_block = lax.optimization_barrier((from_left, from_right, w_block))
    fy_n = lax.axis_size("fy")
    w_left = ring_shift(w_block, "fy", fy_n, 1)
    w_right = ring_shift(w_block, "fy", fy_n, -1)
    cut = pair.shape[3] // 2
    far_low = ring_shift(from_right[..., :cut], "cx", ring, -1)
    far_high = ring_shift(from_left[..., cut:], "cx", ring, 1)
    far_low, far_high, w_left, w_right = lax.optimization_barrier((far_low, far_high, w_left, w_right))
    w_cut = w_block.shape[1] // 2
    w_far_low = ring_shift(w_right[:, :w_cut], "fy", fy_n, -1)
    w_far_high = ring_shift(w_left[:, w_cut:], "fy", fy_n, 1)
    gathered = jnp.concatenate([pair, from_right, far_low, far_high, from_left], axis=3)
    me_fy = lax.axis_index("fy")
    rotate = lax.axis_index("cx")
    w_far = jnp.concatenate([w_far_low, w_far_high], axis=1)
    w_out = jnp.zeros((taps, fy_n) + w_block.shape[1:], w_block.dtype)
    for offset, piece in ((0, w_block), (1, w_right), (2, w_far), (fy_n - 1, w_left)):
        place = (me_fy + offset - rotate + 2 * fy_n) % fy_n
        w_out = lax.dynamic_update_slice(w_out, piece[:, None], (0, place, 0, 0))
    both = xor_stack(w_out, "fc", 1, 2).reshape(taps, -1, w_block.shape[2])
    full_spatial, full_temporal = both[:9], both[9:]
    kernel = full_spatial.reshape((3, 3) + full_spatial.shape[1:])
    spatial = lax.conv_general_dilated(
        gathered,
        kernel,
        (1, 1),
        ((0, 0), (1, 1)),
        dimension_numbers=("NHWC", "HWIO", "NHWC"),
        preferred_element_type=jnp.float32,
    )
    hidden = (spatial + biases[0]).astype(jnp.bfloat16)
    active = jax.nn.silu(hidden.astype(jnp.float32)).astype(jnp.bfloat16)
    index = lax.axis_index(FRAME)
    edge_ids = jnp.full((1,), -1, jnp.int32)
    padded_ids = jnp.concatenate([edge_ids, clip_id, edge_ids])
    local_ids = lax.dynamic_slice_in_dim(padded_ids, index * fr_count, fr_count + 2)
    prev_ok = (local_ids[1:-1] == local_ids[:-2]).astype(jnp.float32).reshape(fr_count, 1, 1, 1)
    next_ok = (local_ids[1:-1] == local_ids[2:]).astype(jnp.float32).reshape(fr_count, 1, 1, 1)
    source = shift_halo(active, FRAME, lax.axis_size(FRAME), 0, 1)
    whole = x_gather(source)
    taps_out = [
        jnp.einsum(
            "fhwc,cd->fhwd",
            whole[tap : tap + fr_count],
            full_temporal[tap],
            preferred_element_type=jnp.float32,
        )
        for tap in range(3)
    ]
    total = (
        hidden.astype(jnp.float32)
        + biases[1]
        + prev_ok * taps_out[0]
        + taps_out[1]
        + next_ok * taps_out[2]
    ).astype(jnp.bfloat16)
    kept = lax.dynamic_slice_in_dim(total, side * col_width, col_width, axis=3)
    given = lax.dynamic_slice_in_dim(total, (1 - side) * col_width, col_width, axis=3)
    returned = lax.ppermute(given, "cz", SWAP)
    return ordered_pair(kept, returned, high, 1)


def solution(mesh):
    frame_n, row_n, col_n = mesh.devices.shape
    fine = Mesh(
        mesh.devices.reshape(frame_n // 2, 2, row_n, col_n // 2, 2),
        ("fy", "fc", "row", "cx", "cz"),
    )
    act = P(FRAME, "row", None, COL)
    weight = P(None, FRAME + ("row",), COL)
    placed = (act, weight, weight, P(COL), P(COL), P())
    return jax.shard_map(body, mesh=fine, in_specs=placed, out_specs=act, check_vma=False)
```

```python
import jax
import jax.numpy as jnp
from jax import lax
from jax.sharding import Mesh
from jax.sharding import PartitionSpec as P

FRAME = ("fy", "fc")
COL = ("cx", "cz")
SWAP = [(0, 1), (1, 0)]


def shift_halo(block, axis, count, dim, width):
    forward = [(i, i + 1) for i in range(count - 1)]
    backward = [(target, source) for source, target in forward]
    low = lax.ppermute(
        lax.slice_in_dim(block, block.shape[dim] - width, None, axis=dim), axis, forward
    )
    high = lax.ppermute(lax.slice_in_dim(block, 0, width, axis=dim), axis, backward)
    return jnp.concatenate([low, block, high], axis=dim)


def ring_shift(block, axis, count, step):
    return lax.ppermute(block, axis, [(i, (i + step) % count) for i in range(count)])


def ordered_pair(own, other, high, dim):
    return jnp.where(
        high, jnp.concatenate([other, own], axis=dim), jnp.concatenate([own, other], axis=dim)
    )


def x_gather(pair):
    ring = lax.axis_size("cx")
    half = pair.shape[3] // 2
    from_left = ring_shift(pair, "cx", ring, 1)
    from_right = ring_shift(pair, "cx", ring, -1)
    far_low = ring_shift(from_right[..., :half], "cx", ring, -1)
    far_high = ring_shift(from_left[..., half:], "cx", ring, 1)
    return jnp.concatenate([pair, from_right, far_low, far_high, from_left], axis=3)


def xor_stack(block, axis, bit, pos):
    count = lax.axis_size(axis)
    other = lax.ppermute(block, axis, [(i, i ^ bit) for i in range(count)])
    high = (lax.axis_index(axis) // bit) % 2 == 1
    return jnp.where(high, jnp.stack([other, block], axis=pos), jnp.stack([block, other], axis=pos))


def body(frames_in, spatial_weight, temporal_weight, spatial_bias, temporal_bias, clip_id):
    fr_count, row_count, wide, col_width = frames_in.shape
    half = row_count // 2
    side = lax.axis_index("cz")
    high = side == 1
    row_n = lax.axis_size("row")
    ring = lax.axis_size("cx")
    weight = jnp.concatenate([spatial_weight, temporal_weight], axis=0)
    taps, depth, _ = weight.shape
    biases = jnp.stack([spatial_bias, temporal_bias])
    biases = ordered_pair(biases, lax.ppermute(biases, "cz", SWAP), high, 1)
    rimmed = shift_halo(frames_in, "row", row_n, 1, 1)
    sent = lax.dynamic_slice_in_dim(frames_in, (1 - side) * (half - 1), half + 1, axis=1)
    partner = lax.ppermute(sent, "cz", SWAP)
    edge = lax.dynamic_slice_in_dim(frames_in, side * (row_count - 1), 1, axis=1)
    diagonal = [(q * 2 + 1, q * 2 + 2) for q in range(row_n - 1)]
    diagonal += [(q * 2, q * 2 - 1) for q in range(1, row_n)]
    rim = lax.ppermute(edge, ("row", "cz"), diagonal)
    w_block = ordered_pair(weight, lax.ppermute(weight, "cz", SWAP), high, 2)
    rimmed, partner, rim, w_block = lax.optimization_barrier((rimmed, partner, rim, w_block))
    mine = lax.dynamic_slice_in_dim(rimmed, side * half, half + 2, axis=1)
    pair = ordered_pair(mine, ordered_pair(rim, partner, high, 1), high, 3)
    from_left = ring_shift(pair, "cx", ring, 1)
    from_right = ring_shift(pair, "cx", ring, -1)
    for pos, bit in enumerate((4, 2, 1)):
        w_block = xor_stack(w_block, "row", bit, 1 + pos)
    w_block = w_block.reshape(taps, row_n * depth, -1)
    from_left, from_right, w_block = lax.optimization_barrier((from_left, from_right, w_block))
    fy_n = lax.axis_size("fy")
    w_left = ring_shift(w_block, "fy", fy_n, 1)
    w_right = ring_shift(w_block, "fy", fy_n, -1)
    cut = pair.shape[3] // 2
    far_low = ring_shift(from_right[..., :cut], "cx", ring, -1)
    far_high = ring_shift(from_left[..., cut:], "cx", ring, 1)
    far_low, far_high, w_left, w_right = lax.optimization_barrier((far_low, far_high, w_left, w_right))
    w_cut = w_block.shape[1] // 2
    w_far_low = ring_shift(w_right[:, :w_cut], "fy", fy_n, -1)
    w_far_high = ring_shift(w_left[:, w_cut:], "fy", fy_n, 1)
    gathered = jnp.concatenate([pair, from_right, far_low, far_high, from_left], axis=3)
    me_fy = lax.axis_index("fy")
    rotate = lax.axis_index("cx")
    w_far = jnp.concatenate([w_far_low, w_far_high], axis=1)
    w_out = jnp.zeros((taps, fy_n) + w_block.shape[1:], w_block.dtype)
    for offset, piece in ((0, w_block), (1, w_right), (2, w_far), (fy_n - 1, w_left)):
        place = (me_fy + offset - rotate + 2 * fy_n) % fy_n
        w_out = lax.dynamic_update_slice(w_out, piece[:, None], (0, place, 0, 0))
    both = xor_stack(w_out, "fc", 1, 2).reshape(taps, -1, w_block.shape[2])
    full_spatial, full_temporal = both[:9], both[9:]
    kernel = full_spatial.reshape((3, 3) + full_spatial.shape[1:])
    spatial = lax.conv_general_dilated(
        gathered,
        kernel,
        (1, 1),
        ((0, 0), (1, 1)),
        dimension_numbers=("NHWC", "HWIO", "NHWC"),
        preferred_element_type=jnp.float32,
    )
    hidden = (spatial + biases[0]).astype(jnp.bfloat16)
    active = jax.nn.silu(hidden.astype(jnp.float32)).astype(jnp.bfloat16)
    index = lax.axis_index(FRAME)
    edge_ids = jnp.full((1,), -1, jnp.int32)
    padded_ids = jnp.concatenate([edge_ids, clip_id, edge_ids])
    local_ids = lax.dynamic_slice_in_dim(padded_ids, index * fr_count, fr_count + 2)
    prev_ok = (local_ids[1:-1] == local_ids[:-2]).astype(jnp.float32).reshape(fr_count, 1, 1, 1)
    next_ok = (local_ids[1:-1] == local_ids[2:]).astype(jnp.float32).reshape(fr_count, 1, 1, 1)
    whole = shift_halo(x_gather(active), FRAME, lax.axis_size(FRAME), 0, 1)
    taps_out = [
        jnp.einsum(
            "fhwc,cd->fhwd",
            whole[tap : tap + fr_count],
            full_temporal[tap],
            preferred_element_type=jnp.float32,
        )
        for tap in range(3)
    ]
    total = (
        hidden.astype(jnp.float32)
        + biases[1]
        + prev_ok * taps_out[0]
        + taps_out[1]
        + next_ok * taps_out[2]
    ).astype(jnp.bfloat16)
    kept = lax.dynamic_slice_in_dim(total, side * col_width, col_width, axis=3)
    given = lax.dynamic_slice_in_dim(total, (1 - side) * col_width, col_width, axis=3)
    returned = lax.ppermute(given, "cz", SWAP)
    return ordered_pair(kept, returned, high, 1)


def solution(mesh):
    frame_n, row_n, col_n = mesh.devices.shape
    fine = Mesh(
        mesh.devices.reshape(frame_n // 2, 2, row_n, col_n // 2, 2),
        ("fy", "fc", "row", "cx", "cz"),
    )
    act = P(FRAME, "row", None, COL)
    weight = P(None, FRAME + ("row",), COL)
    placed = (act, weight, weight, P(COL), P(COL), P())
    return jax.shard_map(body, mesh=fine, in_specs=placed, out_specs=act, check_vma=False)
```

```python
import jax
import jax.numpy as jnp
from jax import lax
from jax.sharding import Mesh
from jax.sharding import PartitionSpec as P

FRAME = ("fy", "fc")
COL = ("cx", "cz")
SWAP = [(0, 1), (1, 0)]


def shift_halo(block, axis, count, dim, width):
    forward = [(i, i + 1) for i in range(count - 1)]
    backward = [(target, source) for source, target in forward]
    low = lax.ppermute(
        lax.slice_in_dim(block, block.shape[dim] - width, None, axis=dim), axis, forward
    )
    high = lax.ppermute(lax.slice_in_dim(block, 0, width, axis=dim), axis, backward)
    return jnp.concatenate([low, block, high], axis=dim)


def ring_shift(block, axis, count, step):
    return lax.ppermute(block, axis, [(i, (i + step) % count) for i in range(count)])


def ordered_pair(own, other, high, dim):
    return jnp.where(
        high, jnp.concatenate([other, own], axis=dim), jnp.concatenate([own, other], axis=dim)
    )


def x_gather(pair):
    ring = lax.axis_size("cx")
    half = pair.shape[3] // 2
    from_left = ring_shift(pair, "cx", ring, 1)
    from_right = ring_shift(pair, "cx", ring, -1)
    far_low = ring_shift(from_right[..., :half], "cx", ring, -1)
    far_high = ring_shift(from_left[..., half:], "cx", ring, 1)
    return jnp.concatenate([pair, from_right, far_low, far_high, from_left], axis=3)


def xor_stack(block, axis, bit, pos):
    count = lax.axis_size(axis)
    other = lax.ppermute(block, axis, [(i, i ^ bit) for i in range(count)])
    high = (lax.axis_index(axis) // bit) % 2 == 1
    return jnp.where(high, jnp.stack([other, block], axis=pos), jnp.stack([block, other], axis=pos))


def body(frames_in, spatial_weight, temporal_weight, spatial_bias, temporal_bias, clip_id):
    fr_count, row_count, wide, col_width = frames_in.shape
    half = row_count // 2
    side = lax.axis_index("cz")
    high = side == 1
    row_n = lax.axis_size("row")
    ring = lax.axis_size("cx")
    weight = jnp.concatenate([spatial_weight, temporal_weight], axis=0)
    taps, depth, _ = weight.shape
    biases = jnp.stack([spatial_bias, temporal_bias])
    biases = ordered_pair(biases, lax.ppermute(biases, "cz", SWAP), high, 1)
    rimmed = shift_halo(frames_in, "row", row_n, 1, 1)
    sent = lax.dynamic_slice_in_dim(frames_in, (1 - side) * (half - 1), half + 1, axis=1)
    edge = lax.dynamic_slice_in_dim(frames_in, side * (row_count - 1), 1, axis=1)
    diagonal = [(q * 2 + 1, q * 2 + 2) for q in range(row_n - 1)]
    diagonal += [(q * 2, q * 2 - 1) for q in range(1, row_n)]
    rim = lax.ppermute(edge, ("row", "cz"), diagonal)
    bounds = (0, fr_count // 2, fr_count // 2 + fr_count // 4, fr_count)
    chunks = []
    chunks.append(lax.ppermute(sent[bounds[0] : bounds[1]], "cz", SWAP))
    w_block = ordered_pair(weight, lax.ppermute(weight, "cz", SWAP), high, 2)
    rimmed, rim, w_block, chunks[0] = lax.optimization_barrier((rimmed, rim, w_block, chunks[0]))
    for pos, bit in enumerate((4, 2)):
        chunk = lax.ppermute(sent[bounds[pos + 1] : bounds[pos + 2]], "cz", SWAP)
        w_block = xor_stack(w_block, "row", bit, 1 + pos)
        chunk, w_block = lax.optimization_barrier((chunk, w_block))
        chunks.append(chunk)
    partner = jnp.concatenate(chunks, axis=0)
    mine = lax.dynamic_slice_in_dim(rimmed, side * half, half + 2, axis=1)
    pair = ordered_pair(mine, ordered_pair(rim, partner, high, 1), high, 3)
    from_left = ring_shift(pair, "cx", ring, 1)
    from_right = ring_shift(pair, "cx", ring, -1)
    w_block = xor_stack(w_block, "row", 1, 3)
    w_block = w_block.reshape(taps, row_n * depth, -1)
    from_left, from_right, w_block = lax.optimization_barrier((from_left, from_right, w_block))
    fy_n = lax.axis_size("fy")
    w_left = ring_shift(w_block, "fy", fy_n, 1)
    w_right = ring_shift(w_block, "fy", fy_n, -1)
    cut = pair.shape[3] // 2
    far_low = ring_shift(from_right[..., :cut], "cx", ring, -1)
    far_high = ring_shift(from_left[..., cut:], "cx", ring, 1)
    far_low, far_high, w_left, w_right = lax.optimization_barrier((far_low, far_high, w_left, w_right))
    w_cut = w_block.shape[1] // 2
    w_far_low = ring_shift(w_right[:, :w_cut], "fy", fy_n, -1)
    w_far_high = ring_shift(w_left[:, w_cut:], "fy", fy_n, 1)
    gathered = jnp.concatenate([pair, from_right, far_low, far_high, from_left], axis=3)
    me_fy = lax.axis_index("fy")
    rotate = lax.axis_index("cx")
    w_far = jnp.concatenate([w_far_low, w_far_high], axis=1)
    w_out = jnp.zeros((taps, fy_n) + w_block.shape[1:], w_block.dtype)
    for offset, piece in ((0, w_block), (1, w_right), (2, w_far), (fy_n - 1, w_left)):
        place = (me_fy + offset - rotate + 2 * fy_n) % fy_n
        w_out = lax.dynamic_update_slice(w_out, piece[:, None], (0, place, 0, 0))
    both = xor_stack(w_out, "fc", 1, 2).reshape(taps, -1, w_block.shape[2])
    full_spatial, full_temporal = both[:9], both[9:]
    kernel = full_spatial.reshape((3, 3) + full_spatial.shape[1:])
    spatial = lax.conv_general_dilated(
        gathered,
        kernel,
        (1, 1),
        ((0, 0), (1, 1)),
        dimension_numbers=("NHWC", "HWIO", "NHWC"),
        preferred_element_type=jnp.float32,
    )
    hidden = (spatial + biases[0]).astype(jnp.bfloat16)
    active = jax.nn.silu(hidden.astype(jnp.float32)).astype(jnp.bfloat16)
    index = lax.axis_index(FRAME)
    edge_ids = jnp.full((1,), -1, jnp.int32)
    padded_ids = jnp.concatenate([edge_ids, clip_id, edge_ids])
    local_ids = lax.dynamic_slice_in_dim(padded_ids, index * fr_count, fr_count + 2)
    prev_ok = (local_ids[1:-1] == local_ids[:-2]).astype(jnp.float32).reshape(fr_count, 1, 1, 1)
    next_ok = (local_ids[1:-1] == local_ids[2:]).astype(jnp.float32).reshape(fr_count, 1, 1, 1)
    whole = shift_halo(x_gather(active), FRAME, lax.axis_size(FRAME), 0, 1)
    taps_out = [
        jnp.einsum(
            "fhwc,cd->fhwd",
            whole[tap : tap + fr_count],
            full_temporal[tap],
            preferred_element_type=jnp.float32,
        )
        for tap in range(3)
    ]
    total = (
        hidden.astype(jnp.float32)
        + biases[1]
        + prev_ok * taps_out[0]
        + taps_out[1]
        + next_ok * taps_out[2]
    ).astype(jnp.bfloat16)
    kept = lax.dynamic_slice_in_dim(total, side * col_width, col_width, axis=3)
    given = lax.dynamic_slice_in_dim(total, (1 - side) * col_width, col_width, axis=3)
    returned = lax.ppermute(given, "cz", SWAP)
    return ordered_pair(kept, returned, high, 1)


def solution(mesh):
    frame_n, row_n, col_n = mesh.devices.shape
    fine = Mesh(
        mesh.devices.reshape(frame_n // 2, 2, row_n, col_n // 2, 2),
        ("fy", "fc", "row", "cx", "cz"),
    )
    act = P(FRAME, "row", None, COL)
    weight = P(None, FRAME + ("row",), COL)
    placed = (act, weight, weight, P(COL), P(COL), P())
    return jax.shard_map(body, mesh=fine, in_specs=placed, out_specs=act, check_vma=False)
```

```python
import jax
import jax.numpy as jnp
from jax import lax
from jax.sharding import Mesh
from jax.sharding import PartitionSpec as P

FRAME = ("fy", "fc")
COL = ("cx", "cz")
SWAP = [(0, 1), (1, 0)]


def shift_halo(block, axis, count, dim, width):
    forward = [(i, i + 1) for i in range(count - 1)]
    backward = [(target, source) for source, target in forward]
    low = lax.ppermute(
        lax.slice_in_dim(block, block.shape[dim] - width, None, axis=dim), axis, forward
    )
    high = lax.ppermute(lax.slice_in_dim(block, 0, width, axis=dim), axis, backward)
    return jnp.concatenate([low, block, high], axis=dim)


def ring_shift(block, axis, count, step):
    return lax.ppermute(block, axis, [(i, (i + step) % count) for i in range(count)])


def ordered_pair(own, other, high, dim):
    return jnp.where(
        high, jnp.concatenate([other, own], axis=dim), jnp.concatenate([own, other], axis=dim)
    )


def x_gather(pair):
    ring = lax.axis_size("cx")
    half = pair.shape[3] // 2
    from_left = ring_shift(pair, "cx", ring, 1)
    from_right = ring_shift(pair, "cx", ring, -1)
    far_low = ring_shift(from_right[..., :half], "cx", ring, -1)
    far_high = ring_shift(from_left[..., half:], "cx", ring, 1)
    return jnp.concatenate([pair, from_right, far_low, far_high, from_left], axis=3)


def xor_stack(block, axis, bit, pos):
    count = lax.axis_size(axis)
    other = lax.ppermute(block, axis, [(i, i ^ bit) for i in range(count)])
    high = (lax.axis_index(axis) // bit) % 2 == 1
    return jnp.where(high, jnp.stack([other, block], axis=pos), jnp.stack([block, other], axis=pos))


def body(frames_in, spatial_weight, temporal_weight, spatial_bias, temporal_bias, clip_id):
    fr_count, row_count, wide, col_width = frames_in.shape
    half = row_count // 2
    side = lax.axis_index("cz")
    high = side == 1
    row_n = lax.axis_size("row")
    ring = lax.axis_size("cx")
    weight = jnp.concatenate([spatial_weight, temporal_weight], axis=0)
    taps, depth, _ = weight.shape
    biases = jnp.stack([spatial_bias, temporal_bias])
    biases = ordered_pair(biases, lax.ppermute(biases, "cz", SWAP), high, 1)
    rimmed = shift_halo(frames_in, "row", row_n, 1, 1)
    sent = lax.dynamic_slice_in_dim(frames_in, (1 - side) * (half - 1), half + 1, axis=1)
    partner = lax.ppermute(sent, "cz", SWAP)
    edge = lax.dynamic_slice_in_dim(frames_in, side * (row_count - 1), 1, axis=1)
    diagonal = [(q * 2 + 1, q * 2 + 2) for q in range(row_n - 1)]
    diagonal += [(q * 2, q * 2 - 1) for q in range(1, row_n)]
    rim = lax.ppermute(edge, ("row", "cz"), diagonal)
    w_block = ordered_pair(weight, lax.ppermute(weight, "cz", SWAP), high, 2)
    rimmed, partner, rim, w_block = lax.optimization_barrier((rimmed, partner, rim, w_block))
    mine = lax.dynamic_slice_in_dim(rimmed, side * half, half + 2, axis=1)
    pair = ordered_pair(mine, ordered_pair(rim, partner, high, 1), high, 3)
    from_left = ring_shift(pair, "cx", ring, 1)
    from_right = ring_shift(pair, "cx", ring, -1)
    for pos, bit in enumerate((4, 2, 1)):
        w_block = xor_stack(w_block, "row", bit, 1 + pos)
    w_block = w_block.reshape(taps, row_n * depth, -1)
    from_left, from_right, w_block = lax.optimization_barrier((from_left, from_right, w_block))
    fy_n = lax.axis_size("fy")
    w_left = ring_shift(w_block, "fy", fy_n, 1)
    w_right = ring_shift(w_block, "fy", fy_n, -1)
    cut = pair.shape[3] // 2
    far_low = ring_shift(from_right[..., :cut], "cx", ring, -1)
    far_high = ring_shift(from_left[..., cut:], "cx", ring, 1)
    w_cut = w_block.shape[1] // 2
    w_far_low = ring_shift(w_right[:, :w_cut], "fy", fy_n, -1)
    w_far_high = ring_shift(w_left[:, w_cut:], "fy", fy_n, 1)
    gathered = jnp.concatenate([pair, from_right, far_low, far_high, from_left], axis=3)
    me_fy = lax.axis_index("fy")
    rotate = lax.axis_index("cx")
    w_far = jnp.concatenate([w_far_low, w_far_high], axis=1)
    w_out = jnp.zeros((taps, fy_n) + w_block.shape[1:], w_block.dtype)
    for offset, piece in ((0, w_block), (1, w_right), (2, w_far), (fy_n - 1, w_left)):
        place = (me_fy + offset - rotate + 2 * fy_n) % fy_n
        w_out = lax.dynamic_update_slice(w_out, piece[:, None], (0, place, 0, 0))
    both = xor_stack(w_out, "fc", 1, 2).reshape(taps, -1, w_block.shape[2])
    full_spatial, full_temporal = both[:9], both[9:]
    kernel = full_spatial.reshape((3, 3) + full_spatial.shape[1:])
    spatial = lax.conv_general_dilated(
        gathered,
        kernel,
        (1, 1),
        ((0, 0), (1, 1)),
        dimension_numbers=("NHWC", "HWIO", "NHWC"),
        preferred_element_type=jnp.float32,
    )
    hidden = (spatial + biases[0]).astype(jnp.bfloat16)
    active = jax.nn.silu(hidden.astype(jnp.float32)).astype(jnp.bfloat16)
    index = lax.axis_index(FRAME)
    edge_ids = jnp.full((1,), -1, jnp.int32)
    padded_ids = jnp.concatenate([edge_ids, clip_id, edge_ids])
    local_ids = lax.dynamic_slice_in_dim(padded_ids, index * fr_count, fr_count + 2)
    prev_ok = (local_ids[1:-1] == local_ids[:-2]).astype(jnp.float32).reshape(fr_count, 1, 1, 1)
    next_ok = (local_ids[1:-1] == local_ids[2:]).astype(jnp.float32).reshape(fr_count, 1, 1, 1)
    whole = shift_halo(x_gather(active), FRAME, lax.axis_size(FRAME), 0, 1)
    taps_out = [
        jnp.einsum(
            "fhwc,cd->fhwd",
            whole[tap : tap + fr_count],
            full_temporal[tap],
            preferred_element_type=jnp.float32,
        )
        for tap in range(3)
    ]
    total = (
        hidden.astype(jnp.float32)
        + biases[1]
        + prev_ok * taps_out[0]
        + taps_out[1]
        + next_ok * taps_out[2]
    ).astype(jnp.bfloat16)
    kept = lax.dynamic_slice_in_dim(total, side * col_width, col_width, axis=3)
    given = lax.dynamic_slice_in_dim(total, (1 - side) * col_width, col_width, axis=3)
    returned = lax.ppermute(given, "cz", SWAP)
    return ordered_pair(kept, returned, high, 1)


def solution(mesh):
    frame_n, row_n, col_n = mesh.devices.shape
    fine = Mesh(
        mesh.devices.reshape(frame_n // 2, 2, row_n, col_n // 2, 2),
        ("fy", "fc", "row", "cx", "cz"),
    )
    act = P(FRAME, "row", None, COL)
    weight = P(None, FRAME + ("row",), COL)
    placed = (act, weight, weight, P(COL), P(COL), P())
    return jax.shard_map(body, mesh=fine, in_specs=placed, out_specs=act, check_vma=False)
```

```python
import jax
import jax.numpy as jnp
from jax import lax
from jax.sharding import Mesh
from jax.sharding import PartitionSpec as P

FRAME = ("fy", "fc")
COL = ("cx", "cz")
SWAP = [(0, 1), (1, 0)]


def shift_halo(block, axis, count, dim, width):
    forward = [(i, i + 1) for i in range(count - 1)]
    backward = [(target, source) for source, target in forward]
    low = lax.ppermute(
        lax.slice_in_dim(block, block.shape[dim] - width, None, axis=dim), axis, forward
    )
    high = lax.ppermute(lax.slice_in_dim(block, 0, width, axis=dim), axis, backward)
    return jnp.concatenate([low, block, high], axis=dim)


def ring_shift(block, axis, count, step):
    return lax.ppermute(block, axis, [(i, (i + step) % count) for i in range(count)])


def ordered_pair(own, other, high, dim):
    return jnp.where(
        high, jnp.concatenate([other, own], axis=dim), jnp.concatenate([own, other], axis=dim)
    )


def x_gather(pair):
    ring = lax.axis_size("cx")
    half = pair.shape[3] // 2
    from_left = ring_shift(pair, "cx", ring, 1)
    from_right = ring_shift(pair, "cx", ring, -1)
    far_low = ring_shift(from_right[..., :half], "cx", ring, -1)
    far_high = ring_shift(from_left[..., half:], "cx", ring, 1)
    return jnp.concatenate([pair, from_right, far_low, far_high, from_left], axis=3)


def xor_stack(block, axis, bit, pos):
    count = lax.axis_size(axis)
    other = lax.ppermute(block, axis, [(i, i ^ bit) for i in range(count)])
    high = (lax.axis_index(axis) // bit) % 2 == 1
    return jnp.where(high, jnp.stack([other, block], axis=pos), jnp.stack([block, other], axis=pos))


def body(frames_in, spatial_weight, temporal_weight, spatial_bias, temporal_bias, clip_id):
    fr_count, row_count, wide, col_width = frames_in.shape
    half = row_count // 2
    side = lax.axis_index("cz")
    high = side == 1
    row_n = lax.axis_size("row")
    ring = lax.axis_size("cx")
    weight = jnp.concatenate([spatial_weight, temporal_weight], axis=0)
    taps, depth, _ = weight.shape
    biases = jnp.stack([spatial_bias, temporal_bias])
    biases = ordered_pair(biases, lax.ppermute(biases, "cz", SWAP), high, 1)
    rimmed = shift_halo(frames_in, "row", row_n, 1, 1)
    sent = lax.dynamic_slice_in_dim(frames_in, (1 - side) * (half - 1), half + 1, axis=1)
    partner = lax.ppermute(sent, "cz", SWAP)
    edge = lax.dynamic_slice_in_dim(frames_in, side * (row_count - 1), 1, axis=1)
    diagonal = [(q * 2 + 1, q * 2 + 2) for q in range(row_n - 1)]
    diagonal += [(q * 2, q * 2 - 1) for q in range(1, row_n)]
    rim = lax.ppermute(edge, ("row", "cz"), diagonal)
    w_block = ordered_pair(weight, lax.ppermute(weight, "cz", SWAP), high, 2)
    rimmed, partner, rim, w_block = lax.optimization_barrier((rimmed, partner, rim, w_block))
    mine = lax.dynamic_slice_in_dim(rimmed, side * half, half + 2, axis=1)
    pair = ordered_pair(mine, ordered_pair(rim, partner, high, 1), high, 3)
    from_left = ring_shift(pair, "cx", ring, 1)
    from_right = ring_shift(pair, "cx", ring, -1)
    for pos, bit in enumerate((4, 2, 1)):
        w_block = xor_stack(w_block, "row", bit, 1 + pos)
    w_block = w_block.reshape(taps, row_n * depth, -1)
    from_left, from_right, w_block = lax.optimization_barrier((from_left, from_right, w_block))
    fy_n = lax.axis_size("fy")
    w_left = ring_shift(w_block, "fy", fy_n, 1)
    w_right = ring_shift(w_block, "fy", fy_n, -1)
    cut = pair.shape[3] // 2
    far_low = ring_shift(from_right[..., :cut], "cx", ring, -1)
    far_high = ring_shift(from_left[..., cut:], "cx", ring, 1)
    far_low, far_high, w_left, w_right = lax.optimization_barrier((far_low, far_high, w_left, w_right))
    w_cut = w_block.shape[1] // 2
    w_far_low = ring_shift(w_block[:, :w_cut], "fy", fy_n, -2)
    w_far_high = ring_shift(w_block[:, w_cut:], "fy", fy_n, 2)
    gathered = jnp.concatenate([pair, from_right, far_low, far_high, from_left], axis=3)
    me_fy = lax.axis_index("fy")
    rotate = lax.axis_index("cx")
    w_far = jnp.concatenate([w_far_low, w_far_high], axis=1)
    w_out = jnp.zeros((taps, fy_n) + w_block.shape[1:], w_block.dtype)
    for offset, piece in ((0, w_block), (1, w_right), (2, w_far), (fy_n - 1, w_left)):
        place = (me_fy + offset - rotate + 2 * fy_n) % fy_n
        w_out = lax.dynamic_update_slice(w_out, piece[:, None], (0, place, 0, 0))
    both = xor_stack(w_out, "fc", 1, 2).reshape(taps, -1, w_block.shape[2])
    full_spatial, full_temporal = both[:9], both[9:]
    kernel = full_spatial.reshape((3, 3) + full_spatial.shape[1:])
    spatial = lax.conv_general_dilated(
        gathered,
        kernel,
        (1, 1),
        ((0, 0), (1, 1)),
        dimension_numbers=("NHWC", "HWIO", "NHWC"),
        preferred_element_type=jnp.float32,
    )
    hidden = (spatial + biases[0]).astype(jnp.bfloat16)
    active = jax.nn.silu(hidden.astype(jnp.float32)).astype(jnp.bfloat16)
    index = lax.axis_index(FRAME)
    edge_ids = jnp.full((1,), -1, jnp.int32)
    padded_ids = jnp.concatenate([edge_ids, clip_id, edge_ids])
    local_ids = lax.dynamic_slice_in_dim(padded_ids, index * fr_count, fr_count + 2)
    prev_ok = (local_ids[1:-1] == local_ids[:-2]).astype(jnp.float32).reshape(fr_count, 1, 1, 1)
    next_ok = (local_ids[1:-1] == local_ids[2:]).astype(jnp.float32).reshape(fr_count, 1, 1, 1)
    whole = shift_halo(x_gather(active), FRAME, lax.axis_size(FRAME), 0, 1)
    taps_out = [
        jnp.einsum(
            "fhwc,cd->fhwd",
            whole[tap : tap + fr_count],
            full_temporal[tap],
            preferred_element_type=jnp.float32,
        )
        for tap in range(3)
    ]
    total = (
        hidden.astype(jnp.float32)
        + biases[1]
        + prev_ok * taps_out[0]
        + taps_out[1]
        + next_ok * taps_out[2]
    ).astype(jnp.bfloat16)
    kept = lax.dynamic_slice_in_dim(total, side * col_width, col_width, axis=3)
    given = lax.dynamic_slice_in_dim(total, (1 - side) * col_width, col_width, axis=3)
    returned = lax.ppermute(given, "cz", SWAP)
    return ordered_pair(kept, returned, high, 1)


def solution(mesh):
    frame_n, row_n, col_n = mesh.devices.shape
    fine = Mesh(
        mesh.devices.reshape(frame_n // 2, 2, row_n, col_n // 2, 2),
        ("fy", "fc", "row", "cx", "cz"),
    )
    act = P(FRAME, "row", None, COL)
    weight = P(None, FRAME + ("row",), COL)
    placed = (act, weight, weight, P(COL), P(COL), P())
    return jax.shard_map(body, mesh=fine, in_specs=placed, out_specs=act, check_vma=False)
```

```python
import jax
import jax.numpy as jnp
from jax import lax
from jax.sharding import Mesh
from jax.sharding import PartitionSpec as P

FRAME = ("fy", "fc")
COL = ("cx", "cz")
SWAP = [(0, 1), (1, 0)]


def shift_halo(block, axis, count, dim, width):
    forward = [(i, i + 1) for i in range(count - 1)]
    backward = [(target, source) for source, target in forward]
    low = lax.ppermute(
        lax.slice_in_dim(block, block.shape[dim] - width, None, axis=dim), axis, forward
    )
    high = lax.ppermute(lax.slice_in_dim(block, 0, width, axis=dim), axis, backward)
    return jnp.concatenate([low, block, high], axis=dim)


def ring_shift(block, axis, count, step):
    return lax.ppermute(block, axis, [(i, (i + step) % count) for i in range(count)])


def ordered_pair(own, other, high, dim):
    return jnp.where(
        high, jnp.concatenate([other, own], axis=dim), jnp.concatenate([own, other], axis=dim)
    )


def x_gather(pair):
    ring = lax.axis_size("cx")
    half = pair.shape[3] // 2
    from_left = ring_shift(pair, "cx", ring, 1)
    from_right = ring_shift(pair, "cx", ring, -1)
    far_low = ring_shift(from_right[..., :half], "cx", ring, -1)
    far_high = ring_shift(from_left[..., half:], "cx", ring, 1)
    return jnp.concatenate([pair, from_right, far_low, far_high, from_left], axis=3)


def xor_stack(block, axis, bit, pos):
    count = lax.axis_size(axis)
    other = lax.ppermute(block, axis, [(i, i ^ bit) for i in range(count)])
    high = (lax.axis_index(axis) // bit) % 2 == 1
    return jnp.where(high, jnp.stack([other, block], axis=pos), jnp.stack([block, other], axis=pos))


def body(frames_in, spatial_weight, temporal_weight, spatial_bias, temporal_bias, clip_id):
    fr_count, row_count, wide, col_width = frames_in.shape
    half = row_count // 2
    side = lax.axis_index("cz")
    high = side == 1
    row_n = lax.axis_size("row")
    ring = lax.axis_size("cx")
    weight = jnp.concatenate([spatial_weight, temporal_weight], axis=0)
    taps, depth, _ = weight.shape
    biases = jnp.stack([spatial_bias, temporal_bias])
    biases = ordered_pair(biases, lax.ppermute(biases, "cz", SWAP), high, 1)
    rimmed = shift_halo(frames_in, "row", row_n, 1, 1)
    sent = lax.dynamic_slice_in_dim(frames_in, (1 - side) * (half - 1), half + 1, axis=1)
    partner = lax.ppermute(sent, "cz", SWAP)
    edge = lax.dynamic_slice_in_dim(frames_in, side * (row_count - 1), 1, axis=1)
    diagonal = [(q * 2 + 1, q * 2 + 2) for q in range(row_n - 1)]
    diagonal += [(q * 2, q * 2 - 1) for q in range(1, row_n)]
    rim = lax.ppermute(edge, ("row", "cz"), diagonal)
    w_block = ordered_pair(weight, lax.ppermute(weight, "cz", SWAP), high, 2)
    rimmed, partner, rim, w_block = lax.optimization_barrier((rimmed, partner, rim, w_block))
    mine = lax.dynamic_slice_in_dim(rimmed, side * half, half + 2, axis=1)
    pair = ordered_pair(mine, ordered_pair(rim, partner, high, 1), high, 3)
    from_left = ring_shift(pair, "cx", ring, 1)
    from_right = ring_shift(pair, "cx", ring, -1)
    for pos, bit in enumerate((4, 2, 1)):
        w_block = xor_stack(w_block, "row", bit, 1 + pos)
    w_block = w_block.reshape(taps, row_n * depth, -1)
    from_left, from_right, w_block = lax.optimization_barrier((from_left, from_right, w_block))
    fy_n = lax.axis_size("fy")
    w_left = ring_shift(w_block, "fy", fy_n, 1)
    w_right = ring_shift(w_block, "fy", fy_n, -1)
    cut = pair.shape[3] // 2
    far_low = ring_shift(from_right[..., :cut], "cx", ring, -1)
    far_high = ring_shift(from_left[..., cut:], "cx", ring, 1)
    far_low, far_high, w_left, w_right = lax.optimization_barrier((far_low, far_high, w_left, w_right))
    w_cut = w_block.shape[1] // 2
    w_far_low = ring_shift(w_right[:, :w_cut], "fy", fy_n, -1)
    w_far_high = ring_shift(w_left[:, w_cut:], "fy", fy_n, 1)
    frame_pos = [(f, c) for f in range(fy_n) for c in range(2)]
    from_up = [((f + 1) % fy_n * 2 + 1 - c, f * 2 + c) for f, c in frame_pos]
    from_down = [((f - 1) % fy_n * 2 + 1 - c, f * 2 + c) for f, c in frame_pos]
    s_far_low = lax.ppermute(w_right[:, :w_cut], FRAME, from_up)
    s_far_high = lax.ppermute(w_left[:, w_cut:], FRAME, from_down)
    held = jnp.stack([w_block, w_right, w_left], axis=1)
    s_held = lax.ppermute(held, "fc", SWAP)
    gathered = jnp.concatenate([pair, from_right, far_low, far_high, from_left], axis=3)
    me_fy = lax.axis_index("fy")
    me_fc = lax.axis_index("fc")
    rotate = lax.axis_index("cx")
    w_far = jnp.concatenate([w_far_low, w_far_high], axis=1)
    s_far = jnp.concatenate([s_far_low, s_far_high], axis=1)
    w_out = jnp.zeros((taps, fy_n, 2) + w_block.shape[1:], w_block.dtype)
    pieces = (
        (0, me_fc, w_block),
        (1, me_fc, w_right),
        (2, me_fc, w_far),
        (fy_n - 1, me_fc, w_left),
        (0, 1 - me_fc, s_held[:, 0]),
        (1, 1 - me_fc, s_held[:, 1]),
        (2, 1 - me_fc, s_far),
        (fy_n - 1, 1 - me_fc, s_held[:, 2]),
    )
    for offset, core, piece in pieces:
        place = (me_fy + offset - rotate + 2 * fy_n) % fy_n
        w_out = lax.dynamic_update_slice(w_out, piece[:, None, None], (0, place, core, 0, 0))
    both = w_out.reshape(taps, -1, w_block.shape[2])
    full_spatial, full_temporal = both[:9], both[9:]
    kernel = full_spatial.reshape((3, 3) + full_spatial.shape[1:])
    spatial = lax.conv_general_dilated(
        gathered,
        kernel,
        (1, 1),
        ((0, 0), (1, 1)),
        dimension_numbers=("NHWC", "HWIO", "NHWC"),
        preferred_element_type=jnp.float32,
    )
    hidden = (spatial + biases[0]).astype(jnp.bfloat16)
    active = jax.nn.silu(hidden.astype(jnp.float32)).astype(jnp.bfloat16)
    index = lax.axis_index(FRAME)
    edge_ids = jnp.full((1,), -1, jnp.int32)
    padded_ids = jnp.concatenate([edge_ids, clip_id, edge_ids])
    local_ids = lax.dynamic_slice_in_dim(padded_ids, index * fr_count, fr_count + 2)
    prev_ok = (local_ids[1:-1] == local_ids[:-2]).astype(jnp.float32).reshape(fr_count, 1, 1, 1)
    next_ok = (local_ids[1:-1] == local_ids[2:]).astype(jnp.float32).reshape(fr_count, 1, 1, 1)
    whole = shift_halo(x_gather(active), FRAME, lax.axis_size(FRAME), 0, 1)
    taps_out = [
        jnp.einsum(
            "fhwc,cd->fhwd",
            whole[tap : tap + fr_count],
            full_temporal[tap],
            preferred_element_type=jnp.float32,
        )
        for tap in range(3)
    ]
    total = (
        hidden.astype(jnp.float32)
        + biases[1]
        + prev_ok * taps_out[0]
        + taps_out[1]
        + next_ok * taps_out[2]
    ).astype(jnp.bfloat16)
    kept = lax.dynamic_slice_in_dim(total, side * col_width, col_width, axis=3)
    given = lax.dynamic_slice_in_dim(total, (1 - side) * col_width, col_width, axis=3)
    returned = lax.ppermute(given, "cz", SWAP)
    return ordered_pair(kept, returned, high, 1)


def solution(mesh):
    frame_n, row_n, col_n = mesh.devices.shape
    fine = Mesh(
        mesh.devices.reshape(frame_n // 2, 2, row_n, col_n // 2, 2),
        ("fy", "fc", "row", "cx", "cz"),
    )
    act = P(FRAME, "row", None, COL)
    weight = P(None, FRAME + ("row",), COL)
    placed = (act, weight, weight, P(COL), P(COL), P())
    return jax.shard_map(body, mesh=fine, in_specs=placed, out_specs=act, check_vma=False)
```

```python
import jax
import jax.numpy as jnp
from jax import lax
from jax.sharding import Mesh
from jax.sharding import PartitionSpec as P

FRAME = ("fy", "fc")
COL = ("cx", "cz")
SWAP = [(0, 1), (1, 0)]


def shift_halo(block, axis, count, dim, width):
    forward = [(i, i + 1) for i in range(count - 1)]
    backward = [(target, source) for source, target in forward]
    low = lax.ppermute(
        lax.slice_in_dim(block, block.shape[dim] - width, None, axis=dim), axis, forward
    )
    high = lax.ppermute(lax.slice_in_dim(block, 0, width, axis=dim), axis, backward)
    return jnp.concatenate([low, block, high], axis=dim)


def ring_shift(block, axis, count, step):
    return lax.ppermute(block, axis, [(i, (i + step) % count) for i in range(count)])


def ordered_pair(own, other, high, dim):
    return jnp.where(
        high, jnp.concatenate([other, own], axis=dim), jnp.concatenate([own, other], axis=dim)
    )


def x_gather(pair):
    ring = lax.axis_size("cx")
    half = pair.shape[3] // 2
    from_left = ring_shift(pair, "cx", ring, 1)
    from_right = ring_shift(pair, "cx", ring, -1)
    far_low = ring_shift(from_right[..., :half], "cx", ring, -1)
    far_high = ring_shift(from_left[..., half:], "cx", ring, 1)
    return jnp.concatenate([pair, from_right, far_low, far_high, from_left], axis=3)


def xor_stack(block, axis, bit, pos):
    count = lax.axis_size(axis)
    other = lax.ppermute(block, axis, [(i, i ^ bit) for i in range(count)])
    high = (lax.axis_index(axis) // bit) % 2 == 1
    return jnp.where(high, jnp.stack([other, block], axis=pos), jnp.stack([block, other], axis=pos))


def body(frames_in, spatial_weight, temporal_weight, spatial_bias, temporal_bias, clip_id):
    fr_count, row_count, wide, col_width = frames_in.shape
    half = row_count // 2
    side = lax.axis_index("cz")
    high = side == 1
    row_n = lax.axis_size("row")
    ring = lax.axis_size("cx")
    weight = jnp.concatenate([spatial_weight, temporal_weight], axis=0)
    taps, depth, _ = weight.shape
    biases = jnp.stack([spatial_bias, temporal_bias])
    biases = ordered_pair(biases, lax.ppermute(biases, "cz", SWAP), high, 1)
    rimmed = shift_halo(frames_in, "row", row_n, 1, 1)
    sent = lax.dynamic_slice_in_dim(frames_in, (1 - side) * (half - 1), half + 1, axis=1)
    partner = lax.ppermute(sent, "cz", SWAP)
    edge = lax.dynamic_slice_in_dim(frames_in, side * (row_count - 1), 1, axis=1)
    diagonal = [(q * 2 + 1, q * 2 + 2) for q in range(row_n - 1)]
    diagonal += [(q * 2, q * 2 - 1) for q in range(1, row_n)]
    rim = lax.ppermute(edge, ("row", "cz"), diagonal)
    far_row = row_n // 2
    cross = [(q * 2 + c, (q ^ far_row) * 2 + 1 - c) for q in range(row_n) for c in range(2)]
    w_cz = lax.ppermute(weight, "cz", SWAP)
    w_row = lax.ppermute(weight, "row", [(q, q ^ far_row) for q in range(row_n)])
    w_cross = lax.ppermute(weight, ("row", "cz"), cross)
    near = ordered_pair(weight, w_cz, high, 2)
    away = ordered_pair(w_row, w_cross, high, 2)
    row_high = (lax.axis_index("row") // far_row) % 2 == 1
    w_block = jnp.where(row_high, jnp.stack([away, near], axis=1), jnp.stack([near, away], axis=1))
    rimmed, partner, rim, w_block = lax.optimization_barrier((rimmed, partner, rim, w_block))
    mine = lax.dynamic_slice_in_dim(rimmed, side * half, half + 2, axis=1)
    pair = ordered_pair(mine, ordered_pair(rim, partner, high, 1), high, 3)
    from_left = ring_shift(pair, "cx", ring, 1)
    from_right = ring_shift(pair, "cx", ring, -1)
    for pos, bit in enumerate((2, 1)):
        w_block = xor_stack(w_block, "row", bit, 2 + pos)
    w_block = w_block.reshape(taps, row_n * depth, -1)
    from_left, from_right, w_block = lax.optimization_barrier((from_left, from_right, w_block))
    fy_n = lax.axis_size("fy")
    w_left = ring_shift(w_block, "fy", fy_n, 1)
    w_right = ring_shift(w_block, "fy", fy_n, -1)
    cut = pair.shape[3] // 2
    far_low = ring_shift(from_right[..., :cut], "cx", ring, -1)
    far_high = ring_shift(from_left[..., cut:], "cx", ring, 1)
    far_low, far_high, w_left, w_right = lax.optimization_barrier((far_low, far_high, w_left, w_right))
    w_cut = w_block.shape[1] // 2
    w_far_low = ring_shift(w_right[:, :w_cut], "fy", fy_n, -1)
    w_far_high = ring_shift(w_left[:, w_cut:], "fy", fy_n, 1)
    frame_pos = [(f, c) for f in range(fy_n) for c in range(2)]
    from_up = [((f + 1) % fy_n * 2 + 1 - c, f * 2 + c) for f, c in frame_pos]
    from_down = [((f - 1) % fy_n * 2 + 1 - c, f * 2 + c) for f, c in frame_pos]
    s_far_low = lax.ppermute(w_right[:, :w_cut], FRAME, from_up)
    s_far_high = lax.ppermute(w_left[:, w_cut:], FRAME, from_down)
    held = jnp.stack([w_block, w_right, w_left], axis=1)
    s_held = lax.ppermute(held, "fc", SWAP)
    gathered = jnp.concatenate([pair, from_right, far_low, far_high, from_left], axis=3)
    me_fy = lax.axis_index("fy")
    me_fc = lax.axis_index("fc")
    rotate = lax.axis_index("cx")
    w_far = jnp.concatenate([w_far_low, w_far_high], axis=1)
    s_far = jnp.concatenate([s_far_low, s_far_high], axis=1)
    w_out = jnp.zeros((taps, fy_n, 2) + w_block.shape[1:], w_block.dtype)
    pieces = (
        (0, me_fc, w_block),
        (1, me_fc, w_right),
        (2, me_fc, w_far),
        (fy_n - 1, me_fc, w_left),
        (0, 1 - me_fc, s_held[:, 0]),
        (1, 1 - me_fc, s_held[:, 1]),
        (2, 1 - me_fc, s_far),
        (fy_n - 1, 1 - me_fc, s_held[:, 2]),
    )
    for offset, core, piece in pieces:
        place = (me_fy + offset - rotate + 2 * fy_n) % fy_n
        w_out = lax.dynamic_update_slice(w_out, piece[:, None, None], (0, place, core, 0, 0))
    both = w_out.reshape(taps, -1, w_block.shape[2])
    full_spatial, full_temporal = both[:9], both[9:]
    kernel = full_spatial.reshape((3, 3) + full_spatial.shape[1:])
    spatial = lax.conv_general_dilated(
        gathered,
        kernel,
        (1, 1),
        ((0, 0), (1, 1)),
        dimension_numbers=("NHWC", "HWIO", "NHWC"),
        preferred_element_type=jnp.float32,
    )
    hidden = (spatial + biases[0]).astype(jnp.bfloat16)
    active = jax.nn.silu(hidden.astype(jnp.float32)).astype(jnp.bfloat16)
    index = lax.axis_index(FRAME)
    edge_ids = jnp.full((1,), -1, jnp.int32)
    padded_ids = jnp.concatenate([edge_ids, clip_id, edge_ids])
    local_ids = lax.dynamic_slice_in_dim(padded_ids, index * fr_count, fr_count + 2)
    prev_ok = (local_ids[1:-1] == local_ids[:-2]).astype(jnp.float32).reshape(fr_count, 1, 1, 1)
    next_ok = (local_ids[1:-1] == local_ids[2:]).astype(jnp.float32).reshape(fr_count, 1, 1, 1)
    whole = shift_halo(x_gather(active), FRAME, lax.axis_size(FRAME), 0, 1)
    taps_out = [
        jnp.einsum(
            "fhwc,cd->fhwd",
            whole[tap : tap + fr_count],
            full_temporal[tap],
            preferred_element_type=jnp.float32,
        )
        for tap in range(3)
    ]
    total = (
        hidden.astype(jnp.float32)
        + biases[1]
        + prev_ok * taps_out[0]
        + taps_out[1]
        + next_ok * taps_out[2]
    ).astype(jnp.bfloat16)
    kept = lax.dynamic_slice_in_dim(total, side * col_width, col_width, axis=3)
    given = lax.dynamic_slice_in_dim(total, (1 - side) * col_width, col_width, axis=3)
    returned = lax.ppermute(given, "cz", SWAP)
    return ordered_pair(kept, returned, high, 1)


def solution(mesh):
    frame_n, row_n, col_n = mesh.devices.shape
    fine = Mesh(
        mesh.devices.reshape(frame_n // 2, 2, row_n, col_n // 2, 2),
        ("fy", "fc", "row", "cx", "cz"),
    )
    act = P(FRAME, "row", None, COL)
    weight = P(None, FRAME + ("row",), COL)
    placed = (act, weight, weight, P(COL), P(COL), P())
    return jax.shard_map(body, mesh=fine, in_specs=placed, out_specs=act, check_vma=False)
```

```python
import jax
import jax.numpy as jnp
from jax import lax
from jax.sharding import Mesh
from jax.sharding import PartitionSpec as P

FRAME = ("fy", "fc")
COL = ("cx", "cz")
SWAP = [(0, 1), (1, 0)]


def shift_halo(block, axis, count, dim, width):
    forward = [(i, i + 1) for i in range(count - 1)]
    backward = [(target, source) for source, target in forward]
    low = lax.ppermute(
        lax.slice_in_dim(block, block.shape[dim] - width, None, axis=dim), axis, forward
    )
    high = lax.ppermute(lax.slice_in_dim(block, 0, width, axis=dim), axis, backward)
    return jnp.concatenate([low, block, high], axis=dim)


def ring_shift(block, axis, count, step):
    return lax.ppermute(block, axis, [(i, (i + step) % count) for i in range(count)])


def ordered_pair(own, other, high, dim):
    return jnp.where(
        high, jnp.concatenate([other, own], axis=dim), jnp.concatenate([own, other], axis=dim)
    )


def x_gather(pair):
    ring = lax.axis_size("cx")
    half = pair.shape[3] // 2
    from_left = ring_shift(pair, "cx", ring, 1)
    from_right = ring_shift(pair, "cx", ring, -1)
    far_low = ring_shift(from_right[..., :half], "cx", ring, -1)
    far_high = ring_shift(from_left[..., half:], "cx", ring, 1)
    return jnp.concatenate([pair, from_right, far_low, far_high, from_left], axis=3)


def xor_stack(block, axis, bit, pos):
    count = lax.axis_size(axis)
    other = lax.ppermute(block, axis, [(i, i ^ bit) for i in range(count)])
    high = (lax.axis_index(axis) // bit) % 2 == 1
    return jnp.where(high, jnp.stack([other, block], axis=pos), jnp.stack([block, other], axis=pos))


def body(frames_in, spatial_weight, temporal_weight, spatial_bias, temporal_bias, clip_id):
    fr_count, row_count, wide, col_width = frames_in.shape
    half = row_count // 2
    side = lax.axis_index("cz")
    high = side == 1
    row_n = lax.axis_size("row")
    ring = lax.axis_size("cx")
    weight = jnp.concatenate([spatial_weight, temporal_weight], axis=0)
    taps, depth, _ = weight.shape
    biases = jnp.stack([spatial_bias, temporal_bias])
    biases = ordered_pair(biases, lax.ppermute(biases, "cz", SWAP), high, 1)
    rimmed = shift_halo(frames_in, "row", row_n, 1, 1)
    sent = lax.dynamic_slice_in_dim(frames_in, (1 - side) * (half - 1), half + 1, axis=1)
    partner = lax.ppermute(sent, "cz", SWAP)
    edge = lax.dynamic_slice_in_dim(frames_in, side * (row_count - 1), 1, axis=1)
    diagonal = [(q * 2 + 1, q * 2 + 2) for q in range(row_n - 1)]
    diagonal += [(q * 2, q * 2 - 1) for q in range(1, row_n)]
    rim = lax.ppermute(edge, ("row", "cz"), diagonal)
    w_block = ordered_pair(weight, lax.ppermute(weight, "cz", SWAP), high, 2)
    rimmed, partner, rim, w_block = lax.optimization_barrier((rimmed, partner, rim, w_block))
    mine = lax.dynamic_slice_in_dim(rimmed, side * half, half + 2, axis=1)
    pair = ordered_pair(mine, ordered_pair(rim, partner, high, 1), high, 3)
    from_left = ring_shift(pair, "cx", ring, 1)
    from_right = ring_shift(pair, "cx", ring, -1)
    for pos, bit in enumerate((4, 2, 1)):
        w_block = xor_stack(w_block, "row", bit, 1 + pos)
    w_block = w_block.reshape(taps, row_n * depth, -1)
    from_left, from_right, w_block = lax.optimization_barrier((from_left, from_right, w_block))
    fy_n = lax.axis_size("fy")
    w_left = ring_shift(w_block, "fy", fy_n, 1)
    w_right = ring_shift(w_block, "fy", fy_n, -1)
    cut = pair.shape[3] // 2
    far_low = ring_shift(from_right[..., :cut], "cx", ring, -1)
    far_high = ring_shift(from_left[..., cut:], "cx", ring, 1)
    far_low, far_high, w_left, w_right = lax.optimization_barrier((far_low, far_high, w_left, w_right))
    w_cut = w_block.shape[1] // 2
    w_far_low = ring_shift(w_right[:, :w_cut], "fy", fy_n, -1)
    w_far_high = ring_shift(w_left[:, w_cut:], "fy", fy_n, 1)
    frame_pos = [(f, c) for f in range(fy_n) for c in range(2)]
    from_up = [((f + 1) % fy_n * 2 + 1 - c, f * 2 + c) for f, c in frame_pos]
    from_down = [((f - 1) % fy_n * 2 + 1 - c, f * 2 + c) for f, c in frame_pos]
    s_far_low = lax.ppermute(w_right[:, :w_cut], FRAME, from_up)
    s_far_high = lax.ppermute(w_left[:, w_cut:], FRAME, from_down)
    held = jnp.stack([w_block, w_right, w_left], axis=1)
    s_held = lax.ppermute(held, "fc", SWAP)
    gathered = jnp.concatenate([pair, from_right, far_low, far_high, from_left], axis=3)
    me_fy = lax.axis_index("fy")
    me_fc = lax.axis_index("fc")
    rotate = lax.axis_index("cx")
    w_far = jnp.concatenate([w_far_low, w_far_high], axis=1)
    s_far = jnp.concatenate([s_far_low, s_far_high], axis=1)
    w_out = jnp.zeros((taps, fy_n, 2) + w_block.shape[1:], w_block.dtype)
    pieces = (
        (0, me_fc, w_block),
        (1, me_fc, w_right),
        (2, me_fc, w_far),
        (fy_n - 1, me_fc, w_left),
        (0, 1 - me_fc, s_held[:, 0]),
        (1, 1 - me_fc, s_held[:, 1]),
        (2, 1 - me_fc, s_far),
        (fy_n - 1, 1 - me_fc, s_held[:, 2]),
    )
    for offset, core, piece in pieces:
        place = (me_fy + offset - rotate + 2 * fy_n) % fy_n
        w_out = lax.dynamic_update_slice(w_out, piece[:, None, None], (0, place, core, 0, 0))
    both = w_out.reshape(taps, -1, w_block.shape[2])
    full_spatial, full_temporal = both[:9], both[9:]
    kernel = full_spatial.reshape((3, 3) + full_spatial.shape[1:])
    spatial = lax.conv_general_dilated(
        gathered,
        kernel,
        (1, 1),
        ((0, 0), (1, 1)),
        dimension_numbers=("NHWC", "HWIO", "NHWC"),
        preferred_element_type=jnp.float32,
    )
    hidden = (spatial + biases[0]).astype(jnp.bfloat16)
    active = jax.nn.silu(hidden.astype(jnp.float32)).astype(jnp.bfloat16)
    index = lax.axis_index(FRAME)
    edge_ids = jnp.full((1,), -1, jnp.int32)
    padded_ids = jnp.concatenate([edge_ids, clip_id, edge_ids])
    local_ids = lax.dynamic_slice_in_dim(padded_ids, index * fr_count, fr_count + 2)
    prev_ok = (local_ids[1:-1] == local_ids[:-2]).astype(jnp.float32).reshape(fr_count, 1, 1, 1)
    next_ok = (local_ids[1:-1] == local_ids[2:]).astype(jnp.float32).reshape(fr_count, 1, 1, 1)
    fr_n = lax.axis_size(FRAME)
    half_c = active.shape[3] // 2
    from_left = ring_shift(active, "cx", ring, 1)
    from_right = ring_shift(active, "cx", ring, -1)
    far_low = ring_shift(from_right[..., :half_c], "cx", ring, -1)
    far_high = ring_shift(from_left[..., half_c:], "cx", ring, 1)
    forward = [(g, g + 1) for g in range(fr_n - 1)]
    backward = [(g + 1, g) for g in range(fr_n - 1)]
    near_last = jnp.concatenate([active[-1:], from_right[-1:], from_left[-1:]], axis=3)
    near_first = jnp.concatenate([active[:1], from_right[:1], from_left[:1]], axis=3)
    low_near = lax.ppermute(near_last, FRAME, forward)
    high_near = lax.ppermute(near_first, FRAME, backward)
    axes = FRAME + ("row", "cx")

    def diagonal(step_f, step_x):
        first = 1 if step_f < 0 else 0
        return [
            ((g * row_n + r) * ring + x, ((g + step_f) * row_n + r) * ring + (x + step_x) % ring)
            for g in range(first, fr_n - 1 + first)
            for r in range(row_n)
            for x in range(ring)
        ]

    low_a = lax.ppermute(from_right[-1:, ..., :half_c], axes, diagonal(1, -1))
    low_b = lax.ppermute(from_left[-1:, ..., half_c:], axes, diagonal(1, 1))
    high_a = lax.ppermute(from_right[:1, ..., :half_c], axes, diagonal(-1, -1))
    high_b = lax.ppermute(from_left[:1, ..., half_c:], axes, diagonal(-1, 1))
    split = 2 * active.shape[3]
    rim_low = jnp.concatenate([low_near[..., :split], low_a, low_b, low_near[..., split:]], axis=3)
    rim_high = jnp.concatenate([high_near[..., :split], high_a, high_b, high_near[..., split:]], axis=3)
    own = jnp.concatenate([active, from_right, far_low, far_high, from_left], axis=3)
    whole = jnp.concatenate([rim_low, own, rim_high], axis=0)
    taps_out = [
        jnp.einsum(
            "fhwc,cd->fhwd",
            whole[tap : tap + fr_count],
            full_temporal[tap],
            preferred_element_type=jnp.float32,
        )
        for tap in range(3)
    ]
    total = (
        hidden.astype(jnp.float32)
        + biases[1]
        + prev_ok * taps_out[0]
        + taps_out[1]
        + next_ok * taps_out[2]
    ).astype(jnp.bfloat16)
    kept = lax.dynamic_slice_in_dim(total, side * col_width, col_width, axis=3)
    given = lax.dynamic_slice_in_dim(total, (1 - side) * col_width, col_width, axis=3)
    returned = lax.ppermute(given, "cz", SWAP)
    return ordered_pair(kept, returned, high, 1)


def solution(mesh):
    frame_n, row_n, col_n = mesh.devices.shape
    fine = Mesh(
        mesh.devices.reshape(frame_n // 2, 2, row_n, col_n // 2, 2),
        ("fy", "fc", "row", "cx", "cz"),
    )
    act = P(FRAME, "row", None, COL)
    weight = P(None, FRAME + ("row",), COL)
    placed = (act, weight, weight, P(COL), P(COL), P())
    return jax.shard_map(body, mesh=fine, in_specs=placed, out_specs=act, check_vma=False)
```

```python
import jax
import jax.numpy as jnp
from jax import lax
from jax.sharding import Mesh
from jax.sharding import PartitionSpec as P

FRAME = ("fy", "fc")
COL = ("cx", "cz")
SWAP = [(0, 1), (1, 0)]


def shift_halo(block, axis, count, dim, width):
    forward = [(i, i + 1) for i in range(count - 1)]
    backward = [(target, source) for source, target in forward]
    low = lax.ppermute(
        lax.slice_in_dim(block, block.shape[dim] - width, None, axis=dim), axis, forward
    )
    high = lax.ppermute(lax.slice_in_dim(block, 0, width, axis=dim), axis, backward)
    return jnp.concatenate([low, block, high], axis=dim)


def ring_shift(block, axis, count, step):
    return lax.ppermute(block, axis, [(i, (i + step) % count) for i in range(count)])


def ordered_pair(own, other, high, dim):
    return jnp.where(
        high, jnp.concatenate([other, own], axis=dim), jnp.concatenate([own, other], axis=dim)
    )


def x_gather(pair):
    ring = lax.axis_size("cx")
    half = pair.shape[3] // 2
    from_left = ring_shift(pair, "cx", ring, 1)
    from_right = ring_shift(pair, "cx", ring, -1)
    far_low = ring_shift(from_right[..., :half], "cx", ring, -1)
    far_high = ring_shift(from_left[..., half:], "cx", ring, 1)
    return jnp.concatenate([pair, from_right, far_low, far_high, from_left], axis=3)


def xor_stack(block, axis, bit, pos):
    count = lax.axis_size(axis)
    other = lax.ppermute(block, axis, [(i, i ^ bit) for i in range(count)])
    high = (lax.axis_index(axis) // bit) % 2 == 1
    return jnp.where(high, jnp.stack([other, block], axis=pos), jnp.stack([block, other], axis=pos))


def body(frames_in, spatial_weight, temporal_weight, spatial_bias, temporal_bias, clip_id):
    fr_count, row_count, wide, col_width = frames_in.shape
    half = row_count // 2
    side = lax.axis_index("cz")
    high = side == 1
    row_n = lax.axis_size("row")
    ring = lax.axis_size("cx")
    weight = jnp.concatenate([spatial_weight, temporal_weight], axis=0)
    taps, depth, _ = weight.shape
    biases = jnp.stack([spatial_bias, temporal_bias])
    biases = ordered_pair(biases, lax.ppermute(biases, "cz", SWAP), high, 1)
    rimmed = shift_halo(frames_in, "row", row_n, 1, 1)
    sent = lax.dynamic_slice_in_dim(frames_in, (1 - side) * (half - 1), half + 1, axis=1)
    partner = lax.ppermute(sent, "cz", SWAP)
    edge = lax.dynamic_slice_in_dim(frames_in, side * (row_count - 1), 1, axis=1)
    diagonal = [(q * 2 + 1, q * 2 + 2) for q in range(row_n - 1)]
    diagonal += [(q * 2, q * 2 - 1) for q in range(1, row_n)]
    rim = lax.ppermute(edge, ("row", "cz"), diagonal)
    w_block = ordered_pair(weight, lax.ppermute(weight, "cz", SWAP), high, 2)
    rimmed, partner, rim, w_block = lax.optimization_barrier((rimmed, partner, rim, w_block))
    mine = lax.dynamic_slice_in_dim(rimmed, side * half, half + 2, axis=1)
    pair = ordered_pair(mine, ordered_pair(rim, partner, high, 1), high, 3)
    from_left = ring_shift(pair, "cx", ring, 1)
    from_right = ring_shift(pair, "cx", ring, -1)
    for pos, bit in enumerate((4, 2, 1)):
        w_block = xor_stack(w_block, "row", bit, 1 + pos)
    w_block = w_block.reshape(taps, row_n * depth, -1)
    cut = pair.shape[3] // 2
    far_low = ring_shift(pair[..., :cut], "cx", ring, -2)
    far_high = ring_shift(pair[..., cut:], "cx", ring, 2)
    from_left, from_right, far_low, far_high, w_block = lax.optimization_barrier(
        (from_left, from_right, far_low, far_high, w_block)
    )
    fy_n = lax.axis_size("fy")
    w_left = ring_shift(w_block, "fy", fy_n, 1)
    w_right = ring_shift(w_block, "fy", fy_n, -1)
    w_left, w_right = lax.optimization_barrier((w_left, w_right))
    w_cut = w_block.shape[1] // 2
    w_far_low = ring_shift(w_right[:, :w_cut], "fy", fy_n, -1)
    w_far_high = ring_shift(w_left[:, w_cut:], "fy", fy_n, 1)
    frame_pos = [(f, c) for f in range(fy_n) for c in range(2)]
    from_up = [((f + 1) % fy_n * 2 + 1 - c, f * 2 + c) for f, c in frame_pos]
    from_down = [((f - 1) % fy_n * 2 + 1 - c, f * 2 + c) for f, c in frame_pos]
    s_far_low = lax.ppermute(w_right[:, :w_cut], FRAME, from_up)
    s_far_high = lax.ppermute(w_left[:, w_cut:], FRAME, from_down)
    held = jnp.stack([w_block, w_right, w_left], axis=1)
    s_held = lax.ppermute(held, "fc", SWAP)
    gathered = jnp.concatenate([pair, from_right, far_low, far_high, from_left], axis=3)
    me_fy = lax.axis_index("fy")
    me_fc = lax.axis_index("fc")
    rotate = lax.axis_index("cx")
    w_far = jnp.concatenate([w_far_low, w_far_high], axis=1)
    s_far = jnp.concatenate([s_far_low, s_far_high], axis=1)
    w_out = jnp.zeros((taps, fy_n, 2) + w_block.shape[1:], w_block.dtype)
    pieces = (
        (0, me_fc, w_block),
        (1, me_fc, w_right),
        (2, me_fc, w_far),
        (fy_n - 1, me_fc, w_left),
        (0, 1 - me_fc, s_held[:, 0]),
        (1, 1 - me_fc, s_held[:, 1]),
        (2, 1 - me_fc, s_far),
        (fy_n - 1, 1 - me_fc, s_held[:, 2]),
    )
    for offset, core, piece in pieces:
        place = (me_fy + offset - rotate + 2 * fy_n) % fy_n
        w_out = lax.dynamic_update_slice(w_out, piece[:, None, None], (0, place, core, 0, 0))
    both = w_out.reshape(taps, -1, w_block.shape[2])
    full_spatial, full_temporal = both[:9], both[9:]
    kernel = full_spatial.reshape((3, 3) + full_spatial.shape[1:])
    spatial = lax.conv_general_dilated(
        gathered,
        kernel,
        (1, 1),
        ((0, 0), (1, 1)),
        dimension_numbers=("NHWC", "HWIO", "NHWC"),
        preferred_element_type=jnp.float32,
    )
    hidden = (spatial + biases[0]).astype(jnp.bfloat16)
    active = jax.nn.silu(hidden.astype(jnp.float32)).astype(jnp.bfloat16)
    index = lax.axis_index(FRAME)
    edge_ids = jnp.full((1,), -1, jnp.int32)
    padded_ids = jnp.concatenate([edge_ids, clip_id, edge_ids])
    local_ids = lax.dynamic_slice_in_dim(padded_ids, index * fr_count, fr_count + 2)
    prev_ok = (local_ids[1:-1] == local_ids[:-2]).astype(jnp.float32).reshape(fr_count, 1, 1, 1)
    next_ok = (local_ids[1:-1] == local_ids[2:]).astype(jnp.float32).reshape(fr_count, 1, 1, 1)
    whole = shift_halo(x_gather(active), FRAME, lax.axis_size(FRAME), 0, 1)
    taps_out = [
        jnp.einsum(
            "fhwc,cd->fhwd",
            whole[tap : tap + fr_count],
            full_temporal[tap],
            preferred_element_type=jnp.float32,
        )
        for tap in range(3)
    ]
    total = (
        hidden.astype(jnp.float32)
        + biases[1]
        + prev_ok * taps_out[0]
        + taps_out[1]
        + next_ok * taps_out[2]
    ).astype(jnp.bfloat16)
    kept = lax.dynamic_slice_in_dim(total, side * col_width, col_width, axis=3)
    given = lax.dynamic_slice_in_dim(total, (1 - side) * col_width, col_width, axis=3)
    returned = lax.ppermute(given, "cz", SWAP)
    return ordered_pair(kept, returned, high, 1)


def solution(mesh):
    frame_n, row_n, col_n = mesh.devices.shape
    fine = Mesh(
        mesh.devices.reshape(frame_n // 2, 2, row_n, col_n // 2, 2),
        ("fy", "fc", "row", "cx", "cz"),
    )
    act = P(FRAME, "row", None, COL)
    weight = P(None, FRAME + ("row",), COL)
    placed = (act, weight, weight, P(COL), P(COL), P())
    return jax.shard_map(body, mesh=fine, in_specs=placed, out_specs=act, check_vma=False)
```

```python
import jax
import jax.numpy as jnp
from jax import lax
from jax.sharding import Mesh
from jax.sharding import PartitionSpec as P

FRAME = ("fy", "fc")
COL = ("cx", "cz")
SWAP = [(0, 1), (1, 0)]


def shift_halo(block, axis, count, dim, width):
    forward = [(i, i + 1) for i in range(count - 1)]
    backward = [(target, source) for source, target in forward]
    low = lax.ppermute(
        lax.slice_in_dim(block, block.shape[dim] - width, None, axis=dim), axis, forward
    )
    high = lax.ppermute(lax.slice_in_dim(block, 0, width, axis=dim), axis, backward)
    return jnp.concatenate([low, block, high], axis=dim)


def ring_shift(block, axis, count, step):
    return lax.ppermute(block, axis, [(i, (i + step) % count) for i in range(count)])


def ordered_pair(own, other, high, dim):
    return jnp.where(
        high, jnp.concatenate([other, own], axis=dim), jnp.concatenate([own, other], axis=dim)
    )


def x_gather(pair):
    ring = lax.axis_size("cx")
    half = pair.shape[3] // 2
    from_left = ring_shift(pair, "cx", ring, 1)
    from_right = ring_shift(pair, "cx", ring, -1)
    far_low = ring_shift(from_right[..., :half], "cx", ring, -1)
    far_high = ring_shift(from_left[..., half:], "cx", ring, 1)
    return jnp.concatenate([pair, from_right, far_low, far_high, from_left], axis=3)


def xor_stack(block, axis, bit, pos):
    count = lax.axis_size(axis)
    other = lax.ppermute(block, axis, [(i, i ^ bit) for i in range(count)])
    high = (lax.axis_index(axis) // bit) % 2 == 1
    return jnp.where(high, jnp.stack([other, block], axis=pos), jnp.stack([block, other], axis=pos))


def body(frames_in, spatial_weight, temporal_weight, spatial_bias, temporal_bias, clip_id):
    fr_count, row_count, wide, col_width = frames_in.shape
    half = row_count // 2
    side = lax.axis_index("cz")
    high = side == 1
    row_n = lax.axis_size("row")
    ring = lax.axis_size("cx")
    weight = jnp.concatenate([spatial_weight, temporal_weight], axis=0)
    taps, depth, _ = weight.shape
    biases = jnp.stack([spatial_bias, temporal_bias])
    biases = ordered_pair(biases, lax.ppermute(biases, "cz", SWAP), high, 1)
    rimmed = shift_halo(frames_in, "row", row_n, 1, 1)
    sent = lax.dynamic_slice_in_dim(frames_in, (1 - side) * (half - 1), half + 1, axis=1)
    partner = lax.ppermute(sent, "cz", SWAP)
    edge = lax.dynamic_slice_in_dim(frames_in, side * (row_count - 1), 1, axis=1)
    diagonal = [(q * 2 + 1, q * 2 + 2) for q in range(row_n - 1)]
    diagonal += [(q * 2, q * 2 - 1) for q in range(1, row_n)]
    rim = lax.ppermute(edge, ("row", "cz"), diagonal)
    w_block = ordered_pair(weight, lax.ppermute(weight, "cz", SWAP), high, 2)
    rimmed, partner, rim, w_block = lax.optimization_barrier((rimmed, partner, rim, w_block))
    mine = lax.dynamic_slice_in_dim(rimmed, side * half, half + 2, axis=1)
    pair = ordered_pair(mine, ordered_pair(rim, partner, high, 1), high, 3)
    from_left = ring_shift(pair, "cx", ring, 1)
    from_right = ring_shift(pair, "cx", ring, -1)
    for pos, bit in enumerate((4, 2, 1)):
        w_block = xor_stack(w_block, "row", bit, 1 + pos)
    w_block = w_block.reshape(taps, row_n * depth, -1)
    from_left, from_right, w_block = lax.optimization_barrier((from_left, from_right, w_block))
    fy_n = lax.axis_size("fy")
    w_left = ring_shift(w_block, "fy", fy_n, 1)
    w_right = ring_shift(w_block, "fy", fy_n, -1)
    cut = pair.shape[3] // 2
    far_low = ring_shift(from_right[..., :cut], "cx", ring, -1)
    far_high = ring_shift(from_left[..., cut:], "cx", ring, 1)
    far_low, far_high, w_left, w_right = lax.optimization_barrier((far_low, far_high, w_left, w_right))
    w_cut = w_block.shape[1] // 2
    w_far_low = ring_shift(w_right[:, :w_cut], "fy", fy_n, -1)
    w_far_high = ring_shift(w_left[:, w_cut:], "fy", fy_n, 1)
    frame_pos = [(f, c) for f in range(fy_n) for c in range(2)]
    from_up = [((f + 1) % fy_n * 2 + 1 - c, f * 2 + c) for f, c in frame_pos]
    from_down = [((f - 1) % fy_n * 2 + 1 - c, f * 2 + c) for f, c in frame_pos]
    s_far_low = lax.ppermute(w_right[:, :w_cut], FRAME, from_up)
    s_far_high = lax.ppermute(w_left[:, w_cut:], FRAME, from_down)
    held = jnp.stack([w_block, w_right, w_left], axis=1)
    s_held = lax.ppermute(held, "fc", SWAP)
    gathered = jnp.concatenate([pair, from_right, far_low, far_high, from_left], axis=3)
    me_fy = lax.axis_index("fy")
    me_fc = lax.axis_index("fc")
    rotate = lax.axis_index("cx")
    w_far = jnp.concatenate([w_far_low, w_far_high], axis=1)
    s_far = jnp.concatenate([s_far_low, s_far_high], axis=1)
    w_outs = [jnp.zeros((count, fy_n, 2) + w_block.shape[1:], w_block.dtype) for count in (9, taps - 9)]
    pieces = (
        (0, me_fc, w_block),
        (1, me_fc, w_right),
        (2, me_fc, w_far),
        (fy_n - 1, me_fc, w_left),
        (0, 1 - me_fc, s_held[:, 0]),
        (1, 1 - me_fc, s_held[:, 1]),
        (2, 1 - me_fc, s_far),
        (fy_n - 1, 1 - me_fc, s_held[:, 2]),
    )
    for offset, core, piece in pieces:
        place = (me_fy + offset - rotate + 2 * fy_n) % fy_n
        for k, (lo, hi) in enumerate(((0, 9), (9, taps))):
            w_outs[k] = lax.dynamic_update_slice(
                w_outs[k], piece[lo:hi, None, None], (0, place, core, 0, 0)
            )
    full_spatial = w_outs[0].reshape(9, -1, w_block.shape[2])
    full_temporal = w_outs[1].reshape(taps - 9, -1, w_block.shape[2])
    kernel = full_spatial.reshape((3, 3) + full_spatial.shape[1:])
    spatial = lax.conv_general_dilated(
        gathered,
        kernel,
        (1, 1),
        ((0, 0), (1, 1)),
        dimension_numbers=("NHWC", "HWIO", "NHWC"),
        preferred_element_type=jnp.float32,
    )
    hidden = (spatial + biases[0]).astype(jnp.bfloat16)
    active = jax.nn.silu(hidden.astype(jnp.float32)).astype(jnp.bfloat16)
    index = lax.axis_index(FRAME)
    edge_ids = jnp.full((1,), -1, jnp.int32)
    padded_ids = jnp.concatenate([edge_ids, clip_id, edge_ids])
    local_ids = lax.dynamic_slice_in_dim(padded_ids, index * fr_count, fr_count + 2)
    prev_ok = (local_ids[1:-1] == local_ids[:-2]).astype(jnp.float32).reshape(fr_count, 1, 1, 1)
    next_ok = (local_ids[1:-1] == local_ids[2:]).astype(jnp.float32).reshape(fr_count, 1, 1, 1)
    whole = shift_halo(x_gather(active), FRAME, lax.axis_size(FRAME), 0, 1)
    taps_out = [
        jnp.einsum(
            "fhwc,cd->fhwd",
            whole[tap : tap + fr_count],
            full_temporal[tap],
            preferred_element_type=jnp.float32,
        )
        for tap in range(3)
    ]
    total = (
        hidden.astype(jnp.float32)
        + biases[1]
        + prev_ok * taps_out[0]
        + taps_out[1]
        + next_ok * taps_out[2]
    ).astype(jnp.bfloat16)
    kept = lax.dynamic_slice_in_dim(total, side * col_width, col_width, axis=3)
    given = lax.dynamic_slice_in_dim(total, (1 - side) * col_width, col_width, axis=3)
    returned = lax.ppermute(given, "cz", SWAP)
    return ordered_pair(kept, returned, high, 1)


def solution(mesh):
    frame_n, row_n, col_n = mesh.devices.shape
    fine = Mesh(
        mesh.devices.reshape(frame_n // 2, 2, row_n, col_n // 2, 2),
        ("fy", "fc", "row", "cx", "cz"),
    )
    act = P(FRAME, "row", None, COL)
    weight = P(None, FRAME + ("row",), COL)
    placed = (act, weight, weight, P(COL), P(COL), P())
    return jax.shard_map(body, mesh=fine, in_specs=placed, out_specs=act, check_vma=False)
```

```python
import jax
import jax.numpy as jnp
from jax import lax
from jax.sharding import Mesh
from jax.sharding import PartitionSpec as P

FRAME = ("fy", "fc")
COL = ("cx", "cz")
SWAP = [(0, 1), (1, 0)]


def shift_halo(block, axis, count, dim, width):
    forward = [(i, i + 1) for i in range(count - 1)]
    backward = [(target, source) for source, target in forward]
    low = lax.ppermute(
        lax.slice_in_dim(block, block.shape[dim] - width, None, axis=dim), axis, forward
    )
    high = lax.ppermute(lax.slice_in_dim(block, 0, width, axis=dim), axis, backward)
    return jnp.concatenate([low, block, high], axis=dim)


def ring_shift(block, axis, count, step):
    return lax.ppermute(block, axis, [(i, (i + step) % count) for i in range(count)])


def ordered_pair(own, other, high, dim):
    return jnp.where(
        high, jnp.concatenate([other, own], axis=dim), jnp.concatenate([own, other], axis=dim)
    )


def x_gather(pair):
    ring = lax.axis_size("cx")
    half = pair.shape[3] // 2
    from_left = ring_shift(pair, "cx", ring, 1)
    from_right = ring_shift(pair, "cx", ring, -1)
    far_low = ring_shift(from_right[..., :half], "cx", ring, -1)
    far_high = ring_shift(from_left[..., half:], "cx", ring, 1)
    return jnp.concatenate([pair, from_right, far_low, far_high, from_left], axis=3)


def xor_stack(block, axis, bit, pos):
    count = lax.axis_size(axis)
    other = lax.ppermute(block, axis, [(i, i ^ bit) for i in range(count)])
    high = (lax.axis_index(axis) // bit) % 2 == 1
    return jnp.where(high, jnp.stack([other, block], axis=pos), jnp.stack([block, other], axis=pos))


def body(frames_in, spatial_weight, temporal_weight, spatial_bias, temporal_bias, clip_id):
    fr_count, row_count, wide, col_width = frames_in.shape
    half = row_count // 2
    side = lax.axis_index("cz")
    high = side == 1
    row_n = lax.axis_size("row")
    ring = lax.axis_size("cx")
    weight = jnp.concatenate([spatial_weight, temporal_weight], axis=0)
    taps, depth, _ = weight.shape
    biases = jnp.stack([spatial_bias, temporal_bias])
    biases = ordered_pair(biases, lax.ppermute(biases, "cz", SWAP), high, 1)
    rimmed = shift_halo(frames_in, "row", row_n, 1, 1)
    sent = lax.dynamic_slice_in_dim(frames_in, (1 - side) * (half - 1), half + 1, axis=1)
    partner = lax.ppermute(sent, "cz", SWAP)
    edge = lax.dynamic_slice_in_dim(frames_in, side * (row_count - 1), 1, axis=1)
    diagonal = [(q * 2 + 1, q * 2 + 2) for q in range(row_n - 1)]
    diagonal += [(q * 2, q * 2 - 1) for q in range(1, row_n)]
    rim = lax.ppermute(edge, ("row", "cz"), diagonal)
    w_block = ordered_pair(weight, lax.ppermute(weight, "cz", SWAP), high, 2)
    rimmed, partner, rim, w_block = lax.optimization_barrier((rimmed, partner, rim, w_block))
    mine = lax.dynamic_slice_in_dim(rimmed, side * half, half + 2, axis=1)
    pair = ordered_pair(mine, ordered_pair(rim, partner, high, 1), high, 3)
    from_left = ring_shift(pair, "cx", ring, 1)
    from_right = ring_shift(pair, "cx", ring, -1)
    for pos, bit in enumerate((4, 2, 1)):
        w_block = xor_stack(w_block, "row", bit, 1 + pos)
    w_block = w_block.reshape(taps, row_n * depth, -1)
    from_left, from_right, w_block = lax.optimization_barrier((from_left, from_right, w_block))
    fy_n = lax.axis_size("fy")
    w_left = ring_shift(w_block, "fy", fy_n, 1)
    w_right = ring_shift(w_block, "fy", fy_n, -1)
    cut = pair.shape[3] // 2
    far_low = ring_shift(from_right[..., :cut], "cx", ring, -1)
    far_high = ring_shift(from_left[..., cut:], "cx", ring, 1)
    far_low, far_high, w_left, w_right = lax.optimization_barrier((far_low, far_high, w_left, w_right))
    w_cut = w_block.shape[1] // 2
    w_far_low = ring_shift(w_right[:, :w_cut], "fy", fy_n, -1)
    w_far_high = ring_shift(w_left[:, w_cut:], "fy", fy_n, 1)
    frame_pos = [(f, c) for f in range(fy_n) for c in range(2)]
    from_up = [((f + 1) % fy_n * 2 + 1 - c, f * 2 + c) for f, c in frame_pos]
    from_down = [((f - 1) % fy_n * 2 + 1 - c, f * 2 + c) for f, c in frame_pos]
    s_far_low = lax.ppermute(w_right[:, :w_cut], FRAME, from_up)
    s_far_high = lax.ppermute(w_left[:, w_cut:], FRAME, from_down)
    held = jnp.stack([w_block, w_right, w_left], axis=1)
    s_held = lax.ppermute(held, "fc", SWAP)
    gathered = jnp.concatenate([pair, from_right, far_low, far_high, from_left], axis=3)
    me_fy = lax.axis_index("fy")
    me_fc = lax.axis_index("fc")
    rotate = lax.axis_index("cx")
    w_far = jnp.concatenate([w_far_low, w_far_high], axis=1)
    s_far = jnp.concatenate([s_far_low, s_far_high], axis=1)
    w_outs = [jnp.zeros((count, fy_n, 2) + w_block.shape[1:], w_block.dtype) for count in (9, taps - 9)]
    pieces = (
        (0, me_fc, w_block),
        (1, me_fc, w_right),
        (2, me_fc, w_far),
        (fy_n - 1, me_fc, w_left),
        (0, 1 - me_fc, s_held[:, 0]),
        (1, 1 - me_fc, s_held[:, 1]),
        (2, 1 - me_fc, s_far),
        (fy_n - 1, 1 - me_fc, s_held[:, 2]),
    )
    for offset, core, piece in pieces:
        place = (me_fy + offset - rotate + 2 * fy_n) % fy_n
        for k, (lo, hi) in enumerate(((0, 9), (9, taps))):
            w_outs[k] = lax.dynamic_update_slice(
                w_outs[k], piece[lo:hi, None, None], (0, place, core, 0, 0)
            )
    full_spatial = w_outs[0].reshape(9, -1, w_block.shape[2])
    full_temporal = w_outs[1].reshape(taps - 9, -1, w_block.shape[2])
    kernel = full_spatial.reshape((3, 3) + full_spatial.shape[1:])
    spatial = lax.conv_general_dilated(
        gathered,
        kernel,
        (1, 1),
        ((0, 0), (1, 1)),
        dimension_numbers=("NHWC", "HWIO", "NHWC"),
        preferred_element_type=jnp.float32,
    )
    hidden = (spatial + biases[0]).astype(jnp.bfloat16)
    active = jax.nn.silu(hidden.astype(jnp.float32)).astype(jnp.bfloat16)
    index = lax.axis_index(FRAME)
    edge_ids = jnp.full((1,), -1, jnp.int32)
    padded_ids = jnp.concatenate([edge_ids, clip_id, edge_ids])
    local_ids = lax.dynamic_slice_in_dim(padded_ids, index * fr_count, fr_count + 2)
    prev_ok = (local_ids[1:-1] == local_ids[:-2]).astype(jnp.float32).reshape(fr_count, 1, 1, 1)
    next_ok = (local_ids[1:-1] == local_ids[2:]).astype(jnp.float32).reshape(fr_count, 1, 1, 1)
    whole = shift_halo(x_gather(active), FRAME, lax.axis_size(FRAME), 0, 1)
    def block_out(start):
        cols = [lax.dynamic_slice_in_dim(full_temporal[tap], start, col_width, axis=1) for tap in range(3)]
        terms = [
            jnp.einsum(
                "fhwc,cd->fhwd",
                whole[tap : tap + fr_count],
                cols[tap],
                preferred_element_type=jnp.float32,
            )
            for tap in range(3)
        ]
        base = lax.dynamic_slice_in_dim(hidden, start, col_width, axis=3).astype(jnp.float32)
        bias = lax.dynamic_slice_in_dim(biases[1], start, col_width, axis=0)
        return (base + bias + prev_ok * terms[0] + terms[1] + next_ok * terms[2]).astype(jnp.bfloat16)

    given = block_out((1 - side) * col_width)
    returned = lax.ppermute(given, "cz", SWAP)
    kept = block_out(side * col_width)
    return ordered_pair(kept, returned, high, 1)


def solution(mesh):
    frame_n, row_n, col_n = mesh.devices.shape
    fine = Mesh(
        mesh.devices.reshape(frame_n // 2, 2, row_n, col_n // 2, 2),
        ("fy", "fc", "row", "cx", "cz"),
    )
    act = P(FRAME, "row", None, COL)
    weight = P(None, FRAME + ("row",), COL)
    placed = (act, weight, weight, P(COL), P(COL), P())
    return jax.shard_map(body, mesh=fine, in_specs=placed, out_specs=act, check_vma=False)
```

```python
import jax
import jax.numpy as jnp
from jax import lax
from jax.sharding import Mesh
from jax.sharding import PartitionSpec as P

FRAME = ("fy", "fc")
COL = ("cx", "cz")
SWAP = [(0, 1), (1, 0)]


def shift_halo(block, axis, count, dim, width):
    forward = [(i, i + 1) for i in range(count - 1)]
    backward = [(target, source) for source, target in forward]
    low = lax.ppermute(
        lax.slice_in_dim(block, block.shape[dim] - width, None, axis=dim), axis, forward
    )
    high = lax.ppermute(lax.slice_in_dim(block, 0, width, axis=dim), axis, backward)
    return jnp.concatenate([low, block, high], axis=dim)


def ring_shift(block, axis, count, step):
    return lax.ppermute(block, axis, [(i, (i + step) % count) for i in range(count)])


def ordered_pair(own, other, high, dim):
    return jnp.where(
        high, jnp.concatenate([other, own], axis=dim), jnp.concatenate([own, other], axis=dim)
    )


def x_gather(pair):
    ring = lax.axis_size("cx")
    half = pair.shape[3] // 2
    from_left = ring_shift(pair, "cx", ring, 1)
    from_right = ring_shift(pair, "cx", ring, -1)
    far_low = ring_shift(from_right[..., :half], "cx", ring, -1)
    far_high = ring_shift(from_left[..., half:], "cx", ring, 1)
    return jnp.concatenate([pair, from_right, far_low, far_high, from_left], axis=3)


def xor_stack(block, axis, bit, pos):
    count = lax.axis_size(axis)
    other = lax.ppermute(block, axis, [(i, i ^ bit) for i in range(count)])
    high = (lax.axis_index(axis) // bit) % 2 == 1
    return jnp.where(high, jnp.stack([other, block], axis=pos), jnp.stack([block, other], axis=pos))


def body(frames_in, spatial_weight, temporal_weight, spatial_bias, temporal_bias, clip_id):
    fr_count, row_count, wide, col_width = frames_in.shape
    half = row_count // 2
    side = lax.axis_index("cz")
    high = side == 1
    row_n = lax.axis_size("row")
    ring = lax.axis_size("cx")
    weight = jnp.concatenate([spatial_weight, temporal_weight], axis=0)
    taps, depth, _ = weight.shape
    biases = jnp.stack([spatial_bias, temporal_bias])
    biases = ordered_pair(biases, lax.ppermute(biases, "cz", SWAP), high, 1)
    rimmed = shift_halo(frames_in, "row", row_n, 1, 1)
    sent = lax.dynamic_slice_in_dim(frames_in, (1 - side) * (half - 1), half + 1, axis=1)
    partner = lax.ppermute(sent, "cz", SWAP)
    edge = lax.dynamic_slice_in_dim(frames_in, side * (row_count - 1), 1, axis=1)
    diagonal = [(q * 2 + 1, q * 2 + 2) for q in range(row_n - 1)]
    diagonal += [(q * 2, q * 2 - 1) for q in range(1, row_n)]
    rim = lax.ppermute(edge, ("row", "cz"), diagonal)
    w_block = ordered_pair(weight, lax.ppermute(weight, "cz", SWAP), high, 2)
    rimmed, partner, rim, w_block = lax.optimization_barrier((rimmed, partner, rim, w_block))
    mine = lax.dynamic_slice_in_dim(rimmed, side * half, half + 2, axis=1)
    pair = ordered_pair(mine, ordered_pair(rim, partner, high, 1), high, 3)
    from_left = ring_shift(pair, "cx", ring, 1)
    from_right = ring_shift(pair, "cx", ring, -1)
    for pos, bit in enumerate((4, 2, 1)):
        w_block = xor_stack(w_block, "row", bit, 1 + pos)
    w_block = w_block.reshape(taps, row_n * depth, -1)
    from_left, from_right, w_block = lax.optimization_barrier((from_left, from_right, w_block))
    fy_n = lax.axis_size("fy")
    w_left = ring_shift(w_block, "fy", fy_n, 1)
    w_right = ring_shift(w_block, "fy", fy_n, -1)
    cut = pair.shape[3] // 2
    far_low = ring_shift(from_right[..., :cut], "cx", ring, -1)
    far_high = ring_shift(from_left[..., cut:], "cx", ring, 1)
    far_low, far_high, w_left, w_right = lax.optimization_barrier((far_low, far_high, w_left, w_right))
    w_cut = w_block.shape[1] // 2
    w_far_low = ring_shift(w_right[:, :w_cut], "fy", fy_n, -1)
    w_far_high = ring_shift(w_left[:, w_cut:], "fy", fy_n, 1)
    frame_pos = [(f, c) for f in range(fy_n) for c in range(2)]
    from_up = [((f + 1) % fy_n * 2 + 1 - c, f * 2 + c) for f, c in frame_pos]
    from_down = [((f - 1) % fy_n * 2 + 1 - c, f * 2 + c) for f, c in frame_pos]
    s_far_low = lax.ppermute(w_right[:, :w_cut], FRAME, from_up)
    s_far_high = lax.ppermute(w_left[:, w_cut:], FRAME, from_down)
    held = jnp.stack([w_block, w_right, w_left], axis=1)
    s_held = lax.ppermute(held, "fc", SWAP)
    gathered = jnp.concatenate([pair, from_right, far_low, far_high, from_left], axis=3)
    me_fy = lax.axis_index("fy")
    me_fc = lax.axis_index("fc")
    rotate = lax.axis_index("cx")
    w_far = jnp.concatenate([w_far_low, w_far_high], axis=1)
    s_far = jnp.concatenate([s_far_low, s_far_high], axis=1)
    w_outs = [jnp.zeros((count, fy_n, 2) + w_block.shape[1:], w_block.dtype) for count in (9, taps - 9)]
    pieces = (
        (0, me_fc, w_block),
        (1, me_fc, w_right),
        (2, me_fc, w_far),
        (fy_n - 1, me_fc, w_left),
        (0, 1 - me_fc, s_held[:, 0]),
        (1, 1 - me_fc, s_held[:, 1]),
        (2, 1 - me_fc, s_far),
        (fy_n - 1, 1 - me_fc, s_held[:, 2]),
    )
    for offset, core, piece in pieces:
        place = (me_fy + offset - rotate + 2 * fy_n) % fy_n
        for k, (lo, hi) in enumerate(((0, 9), (9, taps))):
            w_outs[k] = lax.dynamic_update_slice(
                w_outs[k], piece[lo:hi, None, None], (0, place, core, 0, 0)
            )
    full_spatial = w_outs[0].reshape(9, -1, w_block.shape[2])
    full_temporal = w_outs[1].reshape(taps - 9, -1, w_block.shape[2])
    kernel = full_spatial.reshape((3, 3) + full_spatial.shape[1:])
    spatial = lax.conv_general_dilated(
        gathered,
        kernel,
        (1, 1),
        ((0, 0), (1, 1)),
        dimension_numbers=("NHWC", "HWIO", "NHWC"),
        preferred_element_type=jnp.float32,
    )
    hidden = (spatial + biases[0]).astype(jnp.bfloat16)
    active = jax.nn.silu(hidden.astype(jnp.float32)).astype(jnp.bfloat16)
    index = lax.axis_index(FRAME)
    edge_ids = jnp.full((1,), -1, jnp.int32)
    padded_ids = jnp.concatenate([edge_ids, clip_id, edge_ids])
    local_ids = lax.dynamic_slice_in_dim(padded_ids, index * fr_count, fr_count + 2)
    prev_ok = (local_ids[1:-1] == local_ids[:-2]).astype(jnp.float32).reshape(fr_count, 1, 1, 1)
    next_ok = (local_ids[1:-1] == local_ids[2:]).astype(jnp.float32).reshape(fr_count, 1, 1, 1)
    own = x_gather(active)
    fr_n = lax.axis_size(FRAME)
    rim_low = lax.ppermute(own[-1:], FRAME, [(g, g + 1) for g in range(fr_n - 1)])
    rim_high = lax.ppermute(own[:1], FRAME, [(g + 1, g) for g in range(fr_n - 1)])

    def apply(frames, tap):
        return jnp.einsum(
            "fhwc,cd->fhwd", frames, full_temporal[tap], preferred_element_type=jnp.float32
        )

    middle = apply(own, 1)
    before = apply(own[:-1], 0)
    after = apply(own[1:], 2)
    taps_out = [
        jnp.concatenate([apply(rim_low, 0), before], axis=0),
        middle,
        jnp.concatenate([after, apply(rim_high, 2)], axis=0),
    ]
    total = (
        hidden.astype(jnp.float32)
        + biases[1]
        + prev_ok * taps_out[0]
        + taps_out[1]
        + next_ok * taps_out[2]
    ).astype(jnp.bfloat16)
    kept = lax.dynamic_slice_in_dim(total, side * col_width, col_width, axis=3)
    given = lax.dynamic_slice_in_dim(total, (1 - side) * col_width, col_width, axis=3)
    returned = lax.ppermute(given, "cz", SWAP)
    return ordered_pair(kept, returned, high, 1)


def solution(mesh):
    frame_n, row_n, col_n = mesh.devices.shape
    fine = Mesh(
        mesh.devices.reshape(frame_n // 2, 2, row_n, col_n // 2, 2),
        ("fy", "fc", "row", "cx", "cz"),
    )
    act = P(FRAME, "row", None, COL)
    weight = P(None, FRAME + ("row",), COL)
    placed = (act, weight, weight, P(COL), P(COL), P())
    return jax.shard_map(body, mesh=fine, in_specs=placed, out_specs=act, check_vma=False)
```
